256 devices in a mesh: row: 32 (over z, x_lo, core), col: 8 (over y, x_hi).
Axes of the slice: x: 4 (x_hi: 2, x_lo: 2; x = x_hi * 2 + x_lo), y: 4, z: 8, core: 2. Of those that a mesh axis runs over, the one named last changes fastest.
Arguments:
- first_homolog_embedding: bfloat16 [128, 1024, 32], P(None, ('row', 'col')), may hold values from -12 to 12
- second_homolog_embedding: bfloat16 [128, 1024, 32], P(None, ('row', 'col')), may hold values from -12 to 12
- token_chain_index: int32 [1024], replicated, may hold values from 0 to 7, never falling along the last dimension, each value on 1 to 384 neighbouring positions
- incoming_pair_state: bfloat16 [1024, 1024, 128], P('row', 'col'), may hold values from -6 to 6
- tensor_mixing_matrix: bfloat16 [1024, 128], replicated, may hold values from -0.1875 to 0.1875
- outer_product_bias: float32 [128], replicated, may hold values from -3 to 3
- transition_norm_gain: float32 [128], replicated, may hold values from 0.5 to 1.5
- transition_gate_weight: bfloat16 [128, 512], replicated, may hold values from -0.5 to 0.5
- transition_up_weight: bfloat16 [128, 512], replicated, may hold values from -0.5 to 0.5
- transition_down_weight: bfloat16 [512, 128], replicated, may hold values from -0.25 to 0.25
- distogram_weight: bfloat16 [128, 64], replicated, may hold values from -0.5 to 0.5
- distogram_bias: float32 [64], replicated, may hold values from -3 to 3
Outputs:
- pair_out: bfloat16 [1024, 1024, 128], P('row', 'col')
- logits: float32 [64, 1024, 1024], P(None, 'row', 'col')
The draws below stay inside these ranges and needn't reach their ends.
Inputs may be any that keep to these rules, and one draw needn't show every extreme that they name: `token_chain_index`: chain numbers never fall along the tokens; each chain has 1 to 384 tokens and one chain has exactly 384.
All inputs are finite; a program needn't handle non-finite values.
Results may differ from the reference program's by a relative error of at most 0.006.
Values may be sent and summed in bfloat16 or wider, within the bound.
No kernel may reach another device: no remote copies, remote signals or barrier semaphores. Data moves between devices by JAX's collectives and lax.ppermute only.
A program may use at most 64 MiB of HBM per device.

```python
import math
import jax
import jax.numpy as jnp
import numpy as np
from jax import lax

FEATURE_DEPTH = 32
EDGE_FEATURES = 128
HID = 512
BINS = 64
SLAB = 64
CHAINS = 8
RESIDUE_WINDOW = 1024
HOMOLOG_NUMBER = 128
LONGEST = 384


def block_levels(rng, shape, shards, low, largest):
    factor_of = 1.0
    for position, blocks in shards:
        heights = jax.random.uniform(jax.random.fold_in(jax.random.fold_in(rng, 6), position), (blocks,), jnp.float32, low / len(shards), largest / len(shards))
        factor_of = factor_of * jnp.repeat(jnp.exp(heights), shape[position] // blocks).reshape((-1,) + (1,) * (len(shape) - 1 - position))
    return factor_of


def length_profile(count, total, limit, slope):
    portions = [(1 << 20) // math.isqrt(rank ** slope) + 1 for rank in range(2, count + 1)]
    rest, counts = total - limit - (count - 1), [1] * (count - 1)
    while rest > 0:
        movable = [i for i in range(count - 1) if counts[i] < limit]
        whole, budget = sum([portions[i] for i in movable]), rest
        for i in movable:
            more = min(limit - counts[i], max(1, budget * portions[i] // whole), rest)
            counts[i] = counts[i] + more
            rest = rest - more
    return np.array([limit] + counts)


def uneven(own_key, number_of, total, most, slope):
    if number_of == 2:
        one = jax.random.randint(own_key, (), max(1, total - most), min(most, total - 1) + 1)
        return jnp.stack([one, total - one])
    sizes = jnp.asarray(length_profile(number_of, total, most, slope), jnp.int32)
    couples = (number_of - 1) // 2
    source_of, receiver = sizes[1:1 + 2 * couples:2], sizes[2:2 + 2 * couples:2]
    room = jnp.minimum(source_of - 1, most - receiver)
    passed = jax.random.randint(jax.random.fold_in(own_key, 1), (couples,), 0, 1 << 20) % (room + 1)
    sizes = sizes.at[1:1 + 2 * couples:2].set(source_of - passed).at[2:2 + 2 * couples:2].set(receiver + passed)
    return sizes[jax.random.permutation(jax.random.fold_in(own_key, 2), number_of)]


def normal_values(own_key, dims, scale, bound, shards=(), held_as=jnp.bfloat16):
    array = scale * jax.random.normal(own_key, dims, jnp.float32)
    if shards:
        array = array * block_levels(own_key, dims, shards, -0.22, 0.18)
    return jnp.clip(array, -bound, bound).astype(held_as)


def setup_inputs(seed: int = 0) -> dict:
    streams_of = jax.random.split(jax.random.key(seed), 13)
    first_homolog_embedding = normal_values(streams_of[0], (HOMOLOG_NUMBER, RESIDUE_WINDOW, FEATURE_DEPTH), 2.0, 12.0, ((1, 256),))
    second_homolog_embedding = normal_values(streams_of[1], (HOMOLOG_NUMBER, RESIDUE_WINDOW, FEATURE_DEPTH), 2.0, 12.0, ((1, 256),))
    token_chain_index = jnp.searchsorted(jnp.cumsum(uneven(streams_of[2], CHAINS, RESIDUE_WINDOW, LONGEST, 2)), jnp.arange(RESIDUE_WINDOW), side="right").astype(jnp.int32)
    incoming_pair_state = normal_values(streams_of[3], (RESIDUE_WINDOW, RESIDUE_WINDOW, EDGE_FEATURES), 1.0, 6.0, ((0, 32), (1, 8)))
    tensor_mixing_matrix = normal_values(streams_of[4], (FEATURE_DEPTH * FEATURE_DEPTH, EDGE_FEATURES), (FEATURE_DEPTH * FEATURE_DEPTH) ** -0.5, 0.1875)
    outer_product_bias = normal_values(streams_of[5], (EDGE_FEATURES,), 0.5, 3.0, (), jnp.float32)
    transition_norm_gain = jnp.clip(1.0 + 0.1 * jax.random.normal(streams_of[6], (EDGE_FEATURES,), jnp.float32), 0.5, 1.5)
    transition_gate_weight = normal_values(streams_of[7], (EDGE_FEATURES, HID), EDGE_FEATURES ** -0.5, 0.5)
    transition_up_weight = normal_values(streams_of[8], (EDGE_FEATURES, HID), EDGE_FEATURES ** -0.5, 0.5)
    transition_down_weight = normal_values(streams_of[9], (HID, EDGE_FEATURES), HID ** -0.5, 0.25)
    distogram_weight = normal_values(streams_of[10], (EDGE_FEATURES, BINS), EDGE_FEATURES ** -0.5, 0.5)
    distogram_bias = normal_values(streams_of[11], (BINS,), 0.5, 3.0, (), jnp.float32)
    return {"first_homolog_embedding": first_homolog_embedding, "second_homolog_embedding": second_homolog_embedding, "token_chain_index": token_chain_index, "incoming_pair_state": incoming_pair_state, "tensor_mixing_matrix": tensor_mixing_matrix, "outer_product_bias": outer_product_bias, "transition_norm_gain": transition_norm_gain, "transition_gate_weight": transition_gate_weight, "transition_up_weight": transition_up_weight, "transition_down_weight": transition_down_weight, "distogram_weight": distogram_weight, "distogram_bias": distogram_bias}


def layer_norm(values, transition_norm_gain):
    center = lax.optimization_barrier(jnp.mean(values, axis=-1, keepdims=True))
    shifted = values - center
    spread = lax.optimization_barrier(jnp.mean(shifted * shifted, axis=-1, keepdims=True))
    return shifted * lax.rsqrt(spread + 1e-05) * transition_norm_gain.astype(jnp.float32)

def transition_rows(mid_rows, transition_norm_gain, transition_gate_weight, transition_up_weight, transition_down_weight):
    mid_float = mid_rows.astype(jnp.float32)
    normed = layer_norm(mid_float, transition_norm_gain).astype(jnp.bfloat16)
    gate_pre = jnp.dot(normed, transition_gate_weight, preferred_element_type=jnp.float32)
    up_pre = jnp.dot(normed, transition_up_weight, preferred_element_type=jnp.float32)
    hidden = (jax.nn.silu(gate_pre) * up_pre).astype(jnp.bfloat16)
    result = mid_float + jnp.dot(hidden, transition_down_weight, preferred_element_type=jnp.float32)
    return result.astype(jnp.bfloat16)

def reference(first_homolog_embedding, second_homolog_embedding, token_chain_index, incoming_pair_state, tensor_mixing_matrix, outer_product_bias, transition_norm_gain, transition_gate_weight, transition_up_weight, transition_down_weight, distogram_weight, distogram_bias):
    grid_piece = 8
    block_count = RESIDUE_WINDOW // grid_piece
    left_single_precision = first_homolog_embedding.astype(jnp.float32)
    right_single_precision = second_homolog_embedding.astype(jnp.float32)

    def pair_block(block_index):
        row_start = (block_index * grid_piece).astype(jnp.int32)
        left_sequence_rows = lax.dynamic_slice_in_dim(left_single_precision, row_start, grid_piece, 1)
        chain_rows = lax.dynamic_slice_in_dim(token_chain_index, row_start, grid_piece, 0)
        same_chain = (chain_rows[:, None] == token_chain_index[None, :]).astype(jnp.float32)
        paired_sum = jnp.einsum('sic,sjd->ijcd', left_sequence_rows[:SLAB], right_single_precision[:SLAB])
        unpaired_sum = jnp.einsum('sic,sjd->ijcd', left_sequence_rows[SLAB:], right_single_precision[SLAB:])
        weight = same_chain[:, :, None, None]
        homolog_mean = (paired_sum + weight * unpaired_sum) / (SLAB * (1.0 + weight))
        raveled_matrix = homolog_mean.astype(jnp.bfloat16).reshape(grid_piece * RESIDUE_WINDOW, FEATURE_DEPTH * FEATURE_DEPTH)
        inputs = lax.dynamic_slice_in_dim(incoming_pair_state, row_start, grid_piece, 0).reshape(grid_piece * RESIDUE_WINDOW, EDGE_FEATURES)
        middle = jnp.dot(raveled_matrix, tensor_mixing_matrix, preferred_element_type=jnp.float32)
        middle = middle + outer_product_bias.astype(jnp.float32) + inputs.astype(jnp.float32)
        middle = middle.astype(jnp.bfloat16)
        updated = transition_rows(middle, transition_norm_gain, transition_gate_weight, transition_up_weight, transition_down_weight)
        projected = jnp.dot(updated, distogram_weight, preferred_element_type=jnp.float32).astype(jnp.bfloat16)
        return (updated.reshape(grid_piece, RESIDUE_WINDOW, EDGE_FEATURES), projected.reshape(grid_piece, RESIDUE_WINDOW, BINS))
    pair_blocks, proj_blocks = lax.map(pair_block, jnp.arange(block_count, dtype=jnp.int32))
    pair_out = pair_blocks.reshape(RESIDUE_WINDOW, RESIDUE_WINDOW, EDGE_FEATURES)
    projected = proj_blocks.reshape(RESIDUE_WINDOW, RESIDUE_WINDOW, BINS)
    logits = jnp.transpose(projected, (2, 0, 1)).astype(jnp.float32)
    logits = logits + jnp.transpose(projected, (2, 1, 0)).astype(jnp.float32)
    logits = logits + distogram_bias.astype(jnp.float32)[:, None, None]
    return (pair_out, logits)
```

```python
import jax
import jax.numpy as jnp
from jax import lax
from jax.experimental import pallas as pl
from jax.experimental.pallas import tpu as pltpu
from jax.sharding import PartitionSpec as P


AXES = ("row", "col")
F32 = jnp.float32
BF16 = jnp.bfloat16
DEVICES = [(a, b, c) for a in range(8) for b in range(4) for c in range(8)]
COL_MASKS = (0, 1, 4, 5, 2, 3, 6, 7)


def flat(a, b, c):
    return (a * 4 + b) * 8 + c


def send(values, target):
    pairs = [(flat(*here), flat(*target(*here))) for here in DEVICES]
    return lax.ppermute(values, AXES, pairs)


def dot_nt(left, right):
    return lax.dot_general(left, right, (((1,), (1,)), ((), ())), preferred_element_type=F32)


def dot_nn(left, right):
    return lax.dot_general(left, right, (((1,), (0,)), ((), ())), preferred_element_type=F32)


def pair_kernel(
    meta,
    left_chunks,
    right_own,
    right_other,
    chain_cols,
    incoming,
    mixing,
    outer_bias,
    gain,
    gate_up,
    down,
    bins,
    eye,
    *rest,
):
    out, keep, give, right, left, outer, tile, rows, sent = rest[-9:]
    core = meta[0]
    z_at = meta[1]
    col_at = meta[2]
    first_chain = meta[4]
    last_chain = meta[4 + 31]

    for step in range(8):
        place = lax.rem(z_at + (step + 4), 8)
        own_row = pl.multiple_of((core * 8 + place) * 128, 128)
        other_row = pl.multiple_of(((1 - core) * 8 + place) * 128, 128)
        right[pl.ds(own_row, 128), :] = right_own[step].astype(F32)
        right[pl.ds(other_row, 128), :] = right_other[step].astype(F32)

    paired = lax.broadcasted_iota(jnp.int32, (64, 128), 1) < 64
    zeros = jnp.zeros((64, 128), BF16)

    def one_chain(chain, carry):
        for step, mask in enumerate(COL_MASKS):
            place = jnp.bitwise_xor(col_at, mask)
            for t in range(4):
                of_row = meta[4 + place * 4 + t]
                values = left_chunks[step, t * 32 : (t + 1) * 32, :]
                values = jnp.where(of_row == chain, values, jnp.zeros_like(values))
                at = pl.multiple_of((place * 2 + t // 2) * 32, 32)
                left[pl.ds(at, 32), (t % 2) * 128 : (t % 2) * 128 + 128] = values
        same = chain_cols[...] == chain
        scale = jnp.where(
            same,
            F32(1.0 / 128.0),
            jnp.where(paired, F32(1.0 / 64.0), F32(0.0)),
        )

        def two_channels(pair, inner):
            blocks = []
            for half in range(2):
                values = (right[pl.ds(pair * 2 + half, 64, stride=32), :] * scale).astype(BF16)
                blocks.append(jnp.concatenate([values, zeros], 1))
                blocks.append(jnp.concatenate([zeros, values], 1))
            product = dot_nt(left[...], jnp.concatenate(blocks, 0)).astype(BF16)

            @pl.when(chain == first_chain)
            def _():
                for ip in range(16):
                    for half in range(2):
                        at = pl.multiple_of((pair * 2 + half) * 32, 32)
                        lanes = (ip % 2) * 128
                        outer[ip // 2, pl.ds(at, 32), lanes : lanes + 128] = product[
                            ip * 32 : (ip + 1) * 32, half * 128 : (half + 1) * 128
                        ]

            @pl.when(chain != first_chain)
            def _():
                for ip in range(16):
                    for half in range(2):
                        at = pl.multiple_of((pair * 2 + half) * 32, 32)
                        lanes = (ip % 2) * 128
                        outer[ip // 2, pl.ds(at, 32), lanes : lanes + 128] += product[
                            ip * 32 : (ip + 1) * 32, half * 128 : (half + 1) * 128
                        ]

            return inner

        return lax.fori_loop(0, 16, two_channels, carry)

    lax.fori_loop(first_chain, last_chain + 1, one_chain, 0)

    def four_rows(quad, carry):
        four = pl.multiple_of(quad * 4, 4)
        arriving = incoming[pl.ds(four, 4)].reshape(256, 128)
        mid = dot_nn(mixing[...], outer[quad]) + dot_nt(eye[...], arriving) + outer_bias[...]
        mid = mid.astype(BF16).astype(F32)
        center = jnp.sum(mid, axis=0, keepdims=True) * F32(1.0 / 128.0)
        shifted = mid - center
        spread = jnp.sum(shifted * shifted, axis=0, keepdims=True) * F32(1.0 / 128.0)
        normed = (shifted * lax.rsqrt(spread + F32(1e-05)) * gain[...]).astype(BF16)
        result = mid
        for part in range(2):
            gate = dot_nn(gate_up[part * 256 : (part + 1) * 256, :], normed)
            up = dot_nn(gate_up[512 + part * 256 : 512 + (part + 1) * 256, :], normed)
            half_gate = gate * F32(0.5)
            hidden = ((half_gate + half_gate * jnp.tanh(half_gate)) * up).astype(BF16)
            result = result + dot_nn(down[:, part * 256 : (part + 1) * 256], hidden)
        turned = jnp.transpose(result.astype(BF16).astype(F32), (1, 0))
        out[pl.ds(four, 4)] = turned.astype(BF16).reshape(4, 64, 128)
        tile[pl.ds(pl.multiple_of(quad * 256, 256), 256), :] = turned
        return carry

    lax.fori_loop(0, 8, four_rows, 0)

    for group in range(8):
        for one in range(8):
            values = tile[pl.ds(group * 8 + one, 32, stride=64), :].astype(BF16)
            rows[group * 32 : (group + 1) * 32, one * 128 : (one + 1) * 128] = values
    sent[...] = dot_nt(rows[...], bins[...]).astype(BF16)
    keep[...] = sent[pl.ds(pl.multiple_of(core * 128, 128), 128), :]
    give[...] = sent[pl.ds(pl.multiple_of((1 - core) * 128, 128), 128), :]


def pair_call(meta, half_at, left, own, other, chain_cols, incoming, weights, so_far):
    whole = lambda shape: pl.BlockSpec(shape, lambda g, m: (0,) * len(shape))
    by_half = pl.BlockSpec((32, 64, 128), lambda g, m: (0, m[3], 0))
    operands = [left, own, other, chain_cols, incoming, *weights]
    specs = [
        whole((8, 128, 128)),
        whole((8, 128, 128)),
        whole((8, 128, 128)),
        pl.BlockSpec((64, 128), lambda g, m: (m[3], 0)),
        by_half,
        *[whole(w.shape) for w in weights],
    ]
    aliases = {}
    if so_far is not None:
        operands.append(so_far)
        specs.append(pl.BlockSpec(memory_space=pl.ANY))
        aliases = {len(operands): 0}
    return pl.pallas_call(
        pair_kernel,
        out_shape=(
            jax.ShapeDtypeStruct((32, 128, 128), BF16),
            jax.ShapeDtypeStruct((128, 512), BF16),
            jax.ShapeDtypeStruct((128, 512), BF16),
        ),
        grid_spec=pltpu.PrefetchScalarGridSpec(
            num_scalar_prefetch=1,
            grid=(1,),
            in_specs=specs,
            out_specs=(by_half, whole((128, 512)), whole((128, 512))),
            scratch_shapes=[
                pltpu.VMEM((2048, 128), F32),
                pltpu.VMEM((512, 256), BF16),
                pltpu.VMEM((8, 1024, 256), BF16),
                pltpu.VMEM((2048, 128), F32),
                pltpu.VMEM((256, 1024), BF16),
                pltpu.VMEM((256, 512), BF16),
            ],
        ),
        input_output_aliases=aliases,
        name="pair_half",
    )(jnp.concatenate([meta[:3], half_at[None], meta[3:]]), *operands)


def own_kernel(tile, bins, bias, out):
    flat_rows = jnp.concatenate([tile[i] for i in range(8)], axis=1)
    product = dot_nt(bins[...], flat_rows).astype(BF16).astype(F32) + bias[...]
    out[...] = product.reshape(64, 8, 128)


def own_call(pair_out, bins, bias):
    return pl.pallas_call(
        own_kernel,
        out_shape=jax.ShapeDtypeStruct((64, 32, 128), F32),
        grid=(4,),
        in_specs=[
            pl.BlockSpec((8, 128, 128), lambda g: (g, 0, 0)),
            pl.BlockSpec((512, 1024), lambda g: (0, 0)),
            pl.BlockSpec((512, 1), lambda g: (0, 0)),
        ],
        out_specs=pl.BlockSpec((64, 8, 128), lambda g: (0, g, 0)),
        name="own_bins",
    )(pair_out, bins, bias)


def join_kernel(meta, own, near, far, eye, out, block):
    b_at = meta[0]
    for source in range(4):
        from_b = jnp.bitwise_xor(b_at, source)
        at = pl.multiple_of(from_b * 32, 32)
        values = near if source < 2 else far
        block[pl.ds(at, 32), :] = values[source % 2, 0]
    for part in range(4):
        turned = dot_nt(eye[...], block[:, part * 128 : (part + 1) * 128])
        out[part * 16 : (part + 1) * 16] = own[part * 16 : (part + 1) * 16] + turned.reshape(
            16, 8, 128
        )


def join_call(b_at, own, near, far, eye):
    arrived = pl.BlockSpec((2, 1, 32, 512), lambda g, m: (0, g, 0, 0))
    piece = pl.BlockSpec((64, 8, 128), lambda g, m: (0, g, 0))
    return pl.pallas_call(
        join_kernel,
        out_shape=jax.ShapeDtypeStruct((64, 32, 128), F32),
        grid_spec=pltpu.PrefetchScalarGridSpec(
            num_scalar_prefetch=1,
            grid=(4,),
            in_specs=[piece, arrived, arrived, pl.BlockSpec((128, 128), lambda g, m: (0, 0))],
            out_specs=piece,
            scratch_shapes=[pltpu.VMEM((128, 512), BF16)],
        ),
        name="join_bins",
    )(b_at[None], own, near, far, eye)


def per_device(
    first_homolog_embedding,
    second_homolog_embedding,
    token_chain_index,
    incoming_pair_state,
    tensor_mixing_matrix,
    outer_product_bias,
    transition_norm_gain,
    transition_gate_weight,
    transition_up_weight,
    transition_down_weight,
    distogram_weight,
    distogram_bias,
):
    row_at = lax.axis_index("row").astype(jnp.int32)
    col_at = lax.axis_index("col").astype(jnp.int32)
    a_at, b_at = row_at // 4, row_at % 4
    x_lo, core = b_at // 2, b_at % 2

    left = jnp.transpose(first_homolog_embedding, (1, 2, 0)).reshape(1, 128, 128)
    right = jnp.transpose(second_homolog_embedding, (1, 2, 0)).reshape(1, 128, 128)

    centre = send(right, lambda a, b, c: (c, b, a))
    left = jnp.concatenate([left, send(left, lambda a, b, c: (a, b, c ^ 1))], 0)
    before = send(centre, lambda a, b, c: ((a + 1) % 8, b, c))
    after = send(centre, lambda a, b, c: ((a - 1) % 8, b, c))
    left = jnp.concatenate([left, send(left, lambda a, b, c: (a, b, c ^ 4))], 0)
    three = jnp.concatenate([before, centre, after], 0)
    low = send(three, lambda a, b, c: ((a + 3) % 8, b, c))
    high = send(three[:2], lambda a, b, c: ((a - 3) % 8, b, c))
    left = jnp.concatenate([left, send(left, lambda a, b, c: (a, b, c ^ 2))], 0)
    own = jnp.concatenate([low, three, high], 0)
    other = send(own, lambda a, b, c: (a, b ^ 1, c))
    own_far = send(own, lambda a, b, c: (a, b ^ 2, c))

    chain_rows = lax.dynamic_slice_in_dim(token_chain_index, row_at * 32, 32, 0)
    chain_cols = lax.dynamic_slice_in_dim(token_chain_index, col_at * 128, 128, 0)
    chain_cols = jnp.broadcast_to(chain_cols[:, None], (128, 128))
    meta = jnp.concatenate([jnp.stack([core, a_at, col_at]), chain_rows])
    eye = jnp.eye(128, dtype=BF16)
    mixing = jnp.transpose(tensor_mixing_matrix.reshape(32, 32, 128), (2, 1, 0)).reshape(128, 1024)
    gate_up = jnp.concatenate([transition_gate_weight.T, transition_up_weight.T], 0)
    bins = (
        distogram_weight.T[:, None, None, :] * jnp.eye(8, dtype=BF16)[None, :, :, None]
    ).reshape(512, 1024)
    weights = [
        mixing,
        outer_product_bias[:, None],
        transition_norm_gain[:, None],
        gate_up,
        transition_down_weight.T,
        bins,
        eye,
    ]

    pair_out, keep, give = pair_call(
        meta, x_lo, left, own, other, chain_cols, incoming_pair_state, weights, None
    )
    other_far = send(own_far, lambda a, b, c: (a, b ^ 1, c))
    near = jnp.stack([keep, send(give, lambda a, b, c: (a, b ^ 1, c))])
    near = send(near, lambda a, b, c: (c, b, a))
    pair_out, keep, give = pair_call(
        meta, 1 - x_lo, left, own_far, other_far, chain_cols, incoming_pair_state, weights, pair_out
    )
    far = jnp.stack([keep, send(give, lambda a, b, c: (a, b ^ 1, c))])
    far = send(far, lambda a, b, c: (c, b ^ 2, a))

    own_bins = own_call(pair_out, bins, jnp.repeat(distogram_bias, 8)[:, None])
    logits = join_call(
        b_at, own_bins, near.reshape(2, 4, 32, 512), far.reshape(2, 4, 32, 512), eye
    )
    return (pair_out, logits)


def solution(mesh):
    placed = (
        P(None, ("row", "col"), None),
        P(None, ("row", "col"), None),
        P(),
        P("row", "col", None),
        P(),
        P(),
        P(),
        P(),
        P(),
        P(),
        P(),
        P(),
    )
    return jax.shard_map(
        per_device,
        mesh=mesh,
        in_specs=placed,
        out_specs=(P("row", "col", None), P(None, "row", "col")),
        check_vma=False,
    )
```

```python
import jax
import jax.numpy as jnp
from jax import lax
from jax.experimental import pallas as pl
from jax.experimental.pallas import tpu as pltpu
from jax.sharding import PartitionSpec as P


AXES = ("row", "col")
F32 = jnp.float32
BF16 = jnp.bfloat16
DEVICES = [(a, b, c) for a in range(8) for b in range(4) for c in range(8)]
COL_MASKS = (0, 1, 4, 5, 2, 3, 6, 7)
UNROLL_D = 2
UNROLL_Q = 2


def flat(a, b, c):
    return (a * 4 + b) * 8 + c


def send(values, target):
    pairs = [(flat(*here), flat(*target(*here))) for here in DEVICES]
    return lax.ppermute(values, AXES, pairs)


def dot_nt(left, right):
    return lax.dot_general(left, right, (((1,), (1,)), ((), ())), preferred_element_type=F32)


def dot_nn(left, right):
    return lax.dot_general(left, right, (((1,), (0,)), ((), ())), preferred_element_type=F32)


def square_eye():
    down = lax.broadcasted_iota(jnp.int32, (128, 128), 0)
    along = lax.broadcasted_iota(jnp.int32, (128, 128), 1)
    return (down == along).astype(F32).astype(BF16)


def turn(values):
    return jnp.transpose(values.astype(F32), (1, 0))


def prep_kernel(
    mix, gate, up, down_w, bins_w, outer_bias, gain, bin_bias,
    mixing, gate_up, down, bins, bias_col, gain_col, bin_col, wide,
):
    wide[...] = mix[...].astype(F32)
    for block in range(8):
        parts = [wide[pl.ds(block * 4 + d, 32, stride=32), :] for d in range(4)]
        mixing[:, block * 128 : (block + 1) * 128] = turn(jnp.concatenate(parts, 0)).astype(BF16)
    for block in range(4):
        lanes = slice(block * 128, (block + 1) * 128)
        gate_up[block * 128 : (block + 1) * 128, :] = turn(gate[:, lanes]).astype(BF16)
        gate_up[512 + block * 128 : 512 + (block + 1) * 128, :] = turn(up[:, lanes]).astype(BF16)
        down[:, lanes] = turn(down_w[lanes, :]).astype(BF16)
    spread = jnp.broadcast_to(bins_w[...].astype(F32)[:, None, :], (64, 8, 128)).reshape(512, 128)
    which = lax.rem(lax.broadcasted_iota(jnp.int32, (512, 128), 0), 8)
    for one in range(8):
        bins[:, one * 128 : (one + 1) * 128] = jnp.where(which == one, spread, 0.0).astype(BF16)
    bias_col[...] = turn(jnp.broadcast_to(outer_bias[...], (128, 128)))
    gain_col[...] = turn(jnp.broadcast_to(gain[...], (128, 128)))
    bin_col[...] = turn(jnp.broadcast_to(bin_bias[...], (128, 64)))


def prep_call(mix, gate, up, down, bins, outer_bias, gain, bin_bias):
    return pl.pallas_call(
        prep_kernel,
        out_shape=(
            jax.ShapeDtypeStruct((128, 1024), BF16),
            jax.ShapeDtypeStruct((1024, 128), BF16),
            jax.ShapeDtypeStruct((128, 512), BF16),
            jax.ShapeDtypeStruct((512, 1024), BF16),
            jax.ShapeDtypeStruct((128, 128), F32),
            jax.ShapeDtypeStruct((128, 128), F32),
            jax.ShapeDtypeStruct((64, 128), F32),
        ),
        scratch_shapes=[pltpu.VMEM((1024, 128), F32)],
        name="prep",
    )(mix, gate, up, down, bins.T, outer_bias[None], gain[None], bin_bias[None])


def pair_kernel(
    meta,
    chain_at,
    left_near,
    left_far,
    right_own,
    right_other,
    chains,
    incoming,
    mixing,
    gate_up,
    down,
    bins,
    bias_col,
    gain_col,
    *rest,
):
    out, keep, give, right, left, outer, tile, rows, sent = rest[-9:]
    row_at, col_at, half_at = meta[0], meta[1], meta[2]
    z_at = lax.div(row_at, 4)
    core = lax.rem(row_at, 2)
    first_chain = chain_at[row_at * 32]
    last_chain = chain_at[row_at * 32 + 31]

    for step in range(8):
        place = lax.rem(z_at + (step + 4), 8)
        own_row = pl.multiple_of((core * 8 + place) * 128, 128)
        other_row = pl.multiple_of(((1 - core) * 8 + place) * 128, 128)
        right[pl.ds(own_row, 128), :] = right_own[step].astype(F32)
        right[pl.ds(other_row, 128), :] = right_other[step].astype(F32)

    paired = lax.broadcasted_iota(jnp.int32, (64, 128), 1) < 64
    token = lax.broadcasted_iota(jnp.int32, (64, 128), 0) + (col_at * 128 + half_at * 64)
    zeros = jnp.zeros((64, 128), BF16)

    def one_chain(chain, add):
        for step, mask in enumerate(COL_MASKS):
            place = jnp.bitwise_xor(col_at, mask)
            chunk = left_near[step] if step < 4 else left_far[step - 4]
            for t in range(4):
                of_row = chain_at[row_at * 32 + place * 4 + t]
                values = chunk[t * 32 : (t + 1) * 32, :]
                values = jnp.where(of_row == chain, values, jnp.zeros_like(values))
                at = pl.multiple_of((place * 2 + t // 2) * 32, 32)
                left[pl.ds(at, 32), (t % 2) * 128 : (t % 2) * 128 + 128] = values
        start = jnp.sum((chains[...] < chain).astype(F32)).astype(jnp.int32)
        stop = jnp.sum((chains[...] <= chain).astype(F32)).astype(jnp.int32)
        same = jnp.logical_and(token >= start, token < stop)
        scale = jnp.where(
            same,
            F32(1.0 / 128.0),
            jnp.where(paired, F32(1.0 / 64.0), F32(0.0)),
        )

        def channels(step, inner):
            weights = []
            for pair in range(UNROLL_D):
                blocks = []
                for half in range(2):
                    d = step * (2 * UNROLL_D) + pair * 2 + half
                    values = (right[pl.ds(d, 64, stride=32), :] * scale).astype(BF16)
                    blocks.append(jnp.concatenate([values, zeros], 1))
                    blocks.append(jnp.concatenate([zeros, values], 1))
                weights.append(jnp.concatenate(blocks, 0))
            for pair in range(UNROLL_D):
                product = dot_nt(left[...], weights[pair]).astype(BF16)
                for ip in range(16):
                    for half in range(2):
                        at = pl.multiple_of((step * (2 * UNROLL_D) + pair * 2 + half) * 32, 32)
                        lanes = (ip % 2) * 128
                        piece = product[ip * 32 : (ip + 1) * 32, half * 128 : (half + 1) * 128]
                        if add:
                            piece = piece + outer[ip // 2, pl.ds(at, 32), lanes : lanes + 128]
                        outer[ip // 2, pl.ds(at, 32), lanes : lanes + 128] = piece
            return inner

        lax.fori_loop(0, 16 // UNROLL_D, channels, 0)

    one_chain(first_chain, False)

    def more_chains(chain, carry):
        one_chain(chain, True)
        return carry

    lax.fori_loop(first_chain + 1, last_chain + 1, more_chains, 0)

    eye = square_eye()
    bias = jnp.concatenate([bias_col[...], bias_col[...]], 1)
    scale_by = jnp.concatenate([gain_col[...], gain_col[...]], 1)

    def some_rows(step, carry):
        quads = [step * UNROLL_Q + q for q in range(UNROLL_Q)]
        mids = []
        for quad in quads:
            arriving = incoming[pl.ds(pl.multiple_of(quad * 4, 4), 4)].reshape(256, 128)
            mid = dot_nn(mixing[...], outer[quad]) + dot_nt(eye, arriving) + bias
            mids.append(mid.astype(BF16).astype(F32))
        normeds = []
        for mid in mids:
            center = jnp.sum(mid, axis=0, keepdims=True) * F32(1.0 / 128.0)
            shifted = mid - center
            spread = jnp.sum(shifted * shifted, axis=0, keepdims=True) * F32(1.0 / 128.0)
            normeds.append((shifted * lax.rsqrt(spread + F32(1e-05)) * scale_by).astype(BF16))
        results = list(mids)
        for part in range(2):
            for q in range(UNROLL_Q):
                gate = dot_nn(gate_up[part * 256 : (part + 1) * 256, :], normeds[q])
                up = dot_nn(gate_up[512 + part * 256 : 512 + (part + 1) * 256, :], normeds[q])
                half_gate = gate * F32(0.5)
                hidden = ((half_gate + half_gate * jnp.tanh(half_gate)) * up).astype(BF16)
                results[q] = results[q] + dot_nn(down[:, part * 256 : (part + 1) * 256], hidden)
        for q, quad in enumerate(quads):
            turned = turn(results[q].astype(BF16))
            out[pl.ds(pl.multiple_of(quad * 4, 4), 4)] = turned.astype(BF16).reshape(4, 64, 128)
            tile[pl.ds(pl.multiple_of(quad * 256, 256), 256), :] = turned
        return carry

    lax.fori_loop(0, 8 // UNROLL_Q, some_rows, 0)

    for group in range(8):
        for one in range(8):
            values = tile[pl.ds(group * 8 + one, 32, stride=64), :].astype(BF16)
            rows[group * 32 : (group + 1) * 32, one * 128 : (one + 1) * 128] = values
    sent[...] = dot_nt(rows[...], bins[...]).astype(BF16)
    keep[...] = sent[pl.ds(pl.multiple_of(core * 128, 128), 128), :]
    give[...] = sent[pl.ds(pl.multiple_of((1 - core) * 128, 128), 128), :]


def pair_call(meta, chain_at, left_near, left_far, own, other, incoming, weights, so_far):
    whole = lambda shape: pl.BlockSpec(shape, lambda g, m, k: (0,) * len(shape))
    by_half = pl.BlockSpec((32, 64, 128), lambda g, m, k: (0, m[2], 0))
    operands = [left_near, left_far, own, other, chain_at.reshape(8, 128), incoming, *weights]
    specs = [
        whole((4, 128, 128)),
        whole((4, 128, 128)),
        whole((8, 128, 128)),
        whole((8, 128, 128)),
        whole((8, 128)),
        by_half,
        *[whole(w.shape) for w in weights],
    ]
    aliases = {}
    if so_far is not None:
        operands.append(so_far)
        specs.append(pl.BlockSpec(memory_space=pl.ANY))
        aliases = {len(operands) + 1: 0}
    return pl.pallas_call(
        pair_kernel,
        out_shape=(
            jax.ShapeDtypeStruct((32, 128, 128), BF16),
            jax.ShapeDtypeStruct((128, 512), BF16),
            jax.ShapeDtypeStruct((128, 512), BF16),
        ),
        grid_spec=pltpu.PrefetchScalarGridSpec(
            num_scalar_prefetch=2,
            grid=(1,),
            in_specs=specs,
            out_specs=(by_half, whole((128, 512)), whole((128, 512))),
            scratch_shapes=[
                pltpu.VMEM((2048, 128), F32),
                pltpu.VMEM((512, 256), BF16),
                pltpu.VMEM((8, 1024, 256), BF16),
                pltpu.VMEM((2048, 128), F32),
                pltpu.VMEM((256, 1024), BF16),
                pltpu.VMEM((256, 512), BF16),
            ],
        ),
        input_output_aliases=aliases,
        name="pair_half",
    )(meta, chain_at, *operands)


def own_kernel(tile, bins, bias, out):
    flat_rows = jnp.concatenate([tile[i] for i in range(8)], axis=1)
    product = dot_nt(bins[...], flat_rows).astype(BF16).astype(F32)
    out[...] = product.reshape(64, 8, 128) + bias[...][:, None, :]


def own_call(pair_out, bins, bias):
    return pl.pallas_call(
        own_kernel,
        out_shape=jax.ShapeDtypeStruct((64, 32, 128), F32),
        grid=(4,),
        in_specs=[
            pl.BlockSpec((8, 128, 128), lambda g: (g, 0, 0)),
            pl.BlockSpec((512, 1024), lambda g: (0, 0)),
            pl.BlockSpec((64, 128), lambda g: (0, 0)),
        ],
        out_specs=pl.BlockSpec((64, 8, 128), lambda g: (0, g, 0)),
        name="own_bins",
    )(pair_out, bins, bias)


def join_kernel(meta, own, near, far, out, block):
    b_at = lax.rem(meta[0], 4)
    eye = square_eye()
    for source in range(4):
        from_b = jnp.bitwise_xor(b_at, source)
        at = pl.multiple_of(from_b * 32, 32)
        values = near if source < 2 else far
        block[pl.ds(at, 32), :] = values[source % 2, 0]
    for part in range(4):
        turned = dot_nt(eye, block[:, part * 128 : (part + 1) * 128])
        out[part * 16 : (part + 1) * 16] = own[part * 16 : (part + 1) * 16] + turned.reshape(
            16, 8, 128
        )


def join_call(meta, own, near, far):
    arrived = pl.BlockSpec((2, 1, 32, 512), lambda g, m: (0, g, 0, 0))
    piece = pl.BlockSpec((64, 8, 128), lambda g, m: (0, g, 0))
    return pl.pallas_call(
        join_kernel,
        out_shape=jax.ShapeDtypeStruct((64, 32, 128), F32),
        grid_spec=pltpu.PrefetchScalarGridSpec(
            num_scalar_prefetch=1,
            grid=(4,),
            in_specs=[piece, arrived, arrived],
            out_specs=piece,
            scratch_shapes=[pltpu.VMEM((128, 512), BF16)],
        ),
        name="join_bins",
    )(meta, own, near, far)


def per_device(
    first_homolog_embedding,
    second_homolog_embedding,
    token_chain_index,
    incoming_pair_state,
    tensor_mixing_matrix,
    outer_product_bias,
    transition_norm_gain,
    transition_gate_weight,
    transition_up_weight,
    transition_down_weight,
    distogram_weight,
    distogram_bias,
):
    row_at = lax.axis_index("row").astype(jnp.int32)
    col_at = lax.axis_index("col").astype(jnp.int32)
    x_lo = (row_at // 2) % 2
    meta_a = jnp.stack([row_at, col_at, x_lo])
    meta_b = jnp.stack([row_at, col_at, 1 - x_lo])

    left = jnp.transpose(first_homolog_embedding, (1, 2, 0)).reshape(1, 128, 128)
    right = jnp.transpose(second_homolog_embedding, (1, 2, 0)).reshape(1, 128, 128)

    centre = send(right, lambda a, b, c: (c, b, a))
    *weights, bin_col = prep_call(
        tensor_mixing_matrix,
        transition_gate_weight,
        transition_up_weight,
        transition_down_weight,
        distogram_weight,
        outer_product_bias,
        transition_norm_gain,
        distogram_bias,
    )
    left_two = jnp.concatenate([left, send(left, lambda a, b, c: (a, b, c ^ 1))], 0)
    before = send(centre, lambda a, b, c: ((a + 1) % 8, b, c))
    after = send(centre, lambda a, b, c: ((a - 1) % 8, b, c))
    left_near = jnp.concatenate([left_two, send(left_two, lambda a, b, c: (a, b, c ^ 4))], 0)
    three = jnp.concatenate([before, centre, after], 0)
    low = send(three, lambda a, b, c: ((a + 3) % 8, b, c))
    high = send(three[:2], lambda a, b, c: ((a - 3) % 8, b, c))
    left_far = send(left_near, lambda a, b, c: (a, b, c ^ 2))
    own = jnp.concatenate([low, three, high], 0)
    other = send(own, lambda a, b, c: (a, b ^ 1, c))
    own_far = send(own, lambda a, b, c: (a, b ^ 2, c))

    pair_out, keep, give = pair_call(
        meta_a, token_chain_index, left_near, left_far, own, other,
        incoming_pair_state, weights, None,
    )
    other_far = send(own_far, lambda a, b, c: (a, b ^ 1, c))
    given = send(give, lambda a, b, c: (a, b ^ 1, c))
    near = send(jnp.stack([keep, given]), lambda a, b, c: (c, b, a))
    pair_out, keep, give = pair_call(
        meta_b, token_chain_index, left_near, left_far, own_far, other_far,
        incoming_pair_state, weights, pair_out,
    )
    given = send(give, lambda a, b, c: (a, b ^ 1, c))
    far = send(jnp.stack([keep, given]), lambda a, b, c: (c, b ^ 2, a))

    own_bins = own_call(pair_out, weights[3], bin_col)
    logits = join_call(meta_a, own_bins, near.reshape(2, 4, 32, 512), far.reshape(2, 4, 32, 512))
    return (pair_out, logits)


def solution(mesh):
    placed = (
        P(None, ("row", "col"), None),
        P(None, ("row", "col"), None),
        P(),
        P("row", "col", None),
        P(),
        P(),
        P(),
        P(),
        P(),
        P(),
        P(),
        P(),
    )
    return jax.shard_map(
        per_device,
        mesh=mesh,
        in_specs=placed,
        out_specs=(P("row", "col", None), P(None, "row", "col")),
        check_vma=False,
    )
```

```python
import functools

import jax
import jax.numpy as jnp
from jax import lax
from jax.experimental import pallas as pl
from jax.experimental.pallas import tpu as pltpu
from jax.sharding import PartitionSpec as P


AXES = ("row", "col")
F32 = jnp.float32
BF16 = jnp.bfloat16
DEVICES = [(a, b, c) for a in range(8) for b in range(4) for c in range(8)]
COL_MASKS = (0, 1, 4, 5, 2, 3, 6, 7)
QUADS = 2


def in_vmem(values):
    return pltpu.with_memory_space_constraint(values, pltpu.VMEM)


VMEM_SPEC = pl.BlockSpec(memory_space=pltpu.VMEM)


def flat(a, b, c):
    return (a * 4 + b) * 8 + c


def send(values, target):
    pairs = [(flat(*here), flat(*target(*here))) for here in DEVICES]
    return lax.ppermute(values, AXES, pairs)


def dot_nt(left, right):
    return lax.dot_general(left, right, (((1,), (1,)), ((), ())), preferred_element_type=F32)


def dot_nn(left, right):
    return lax.dot_general(left, right, (((1,), (0,)), ((), ())), preferred_element_type=F32)


def square_eye():
    down = lax.broadcasted_iota(jnp.int32, (128, 128), 0)
    along = lax.broadcasted_iota(jnp.int32, (128, 128), 1)
    return (down == along).astype(F32).astype(BF16)


def turn(values):
    return jnp.transpose(values.astype(F32), (1, 0))


def prep_kernel(
    mix, gate, up, down_w, bins_w, outer_bias, gain, bin_bias,
    mixing, gate_up, down, bins, bias_col, gain_col, bin_col, wide,
):
    wide[...] = mix[...].astype(F32)
    for block in range(8):
        parts = [wide[pl.ds(block * 4 + d, 32, stride=32), :] for d in range(4)]
        mixing[:, block * 128 : (block + 1) * 128] = turn(jnp.concatenate(parts, 0)).astype(BF16)
    for block in range(4):
        lanes = slice(block * 128, (block + 1) * 128)
        gate_up[block * 128 : (block + 1) * 128, :] = turn(gate[:, lanes]).astype(BF16)
        gate_up[512 + block * 128 : 512 + (block + 1) * 128, :] = turn(up[:, lanes]).astype(BF16)
        down[:, lanes] = turn(down_w[lanes, :]).astype(BF16)
    spread = jnp.broadcast_to(bins_w[...].astype(F32)[:, None, :], (64, 8, 128)).reshape(512, 128)
    which = lax.rem(lax.broadcasted_iota(jnp.int32, (512, 128), 0), 8)
    for one in range(8):
        bins[:, one * 128 : (one + 1) * 128] = jnp.where(which == one, spread, 0.0).astype(BF16)
    bias_col[...] = turn(jnp.broadcast_to(outer_bias[...], (128, 128)))
    gain_col[...] = turn(jnp.broadcast_to(gain[...], (128, 128)))
    bin_col[...] = turn(jnp.broadcast_to(bin_bias[...], (128, 64)))


def prep_call(mix, gate, up, down, bins, outer_bias, gain, bin_bias):
    operands = (mix, gate, up, down, bins.T, outer_bias[None], gain[None], bin_bias[None])
    return pl.pallas_call(
        prep_kernel,
        out_shape=(
            pltpu.VMEM((128, 1024), BF16),
            pltpu.VMEM((1024, 128), BF16),
            pltpu.VMEM((128, 512), BF16),
            pltpu.VMEM((512, 1024), BF16),
            pltpu.VMEM((128, 128), F32),
            pltpu.VMEM((128, 128), F32),
            pltpu.VMEM((64, 128), F32),
        ),
        out_specs=[VMEM_SPEC] * 7,
        scratch_shapes=[pltpu.VMEM((1024, 128), F32)],
        compiler_params=pltpu.CompilerParams(vmem_limit_bytes=16 << 20),
        name="prep",
    )(*[pltpu.with_memory_space_constraint(v, pltpu.HBM) for v in operands])


def half_of(row_at, flip):
    x_lo = lax.rem(lax.div(row_at, 2), 2)
    return 1 - x_lo if flip else x_lo


def pair_kernel(
    meta,
    chain_at,
    left_near,
    left_far,
    right_own,
    right_other,
    chains,
    incoming,
    mixing,
    gate_up,
    down,
    bins,
    bias_col,
    gain_col,
    *rest,
    flip,
):
    out, keep, give, right, left, outer, tile, rows, sent = rest[-9:]
    row_at, col_at = meta[0], meta[1]
    half_at = half_of(row_at, flip)
    z_at = lax.div(row_at, 4)
    core = lax.rem(row_at, 2)
    first_chain = chain_at[row_at * 32]
    last_chain = chain_at[row_at * 32 + 31]

    for step in range(8):
        place = lax.rem(z_at + (step + 4), 8)
        own_row = pl.multiple_of((core * 8 + place) * 128, 128)
        other_row = pl.multiple_of(((1 - core) * 8 + place) * 128, 128)
        right[pl.ds(own_row, 128), :] = right_own[step].astype(F32)
        right[pl.ds(other_row, 128), :] = right_other[step].astype(F32)

    paired = lax.broadcasted_iota(jnp.int32, (64, 128), 1) < 64
    token = lax.broadcasted_iota(jnp.int32, (64, 128), 0) + (col_at * 128 + half_at * 64)
    zeros = jnp.zeros((64, 128), BF16)

    def one_chain(chain, window, unroll):
        for step, mask in enumerate(COL_MASKS):
            place = jnp.bitwise_xor(col_at, mask)
            chunk = left_near[step] if step < 4 else left_far[step - 4]
            for t in range(4):
                of_row = chain_at[row_at * 32 + place * 4 + t]
                values = chunk[t * 32 : (t + 1) * 32, :]
                values = jnp.where(of_row == chain, values, jnp.zeros_like(values))
                at = pl.multiple_of((place * 2 + t // 2) * 32, 32)
                left[pl.ds(at, 32), (t % 2) * 128 : (t % 2) * 128 + 128] = values
        start = jnp.sum((chains[...] < chain).astype(F32)).astype(jnp.int32)
        stop = jnp.sum((chains[...] <= chain).astype(F32)).astype(jnp.int32)
        same = jnp.logical_and(token >= start, token < stop)
        scale = jnp.where(
            same,
            F32(1.0 / 128.0),
            jnp.where(paired, F32(1.0 / 64.0), F32(0.0)),
        )

        def channels(step, inner):
            weights = []
            for pair in range(unroll):
                blocks = []
                for half in range(2):
                    d = step * (2 * unroll) + pair * 2 + half
                    values = (right[pl.ds(d, 64, stride=32), :] * scale).astype(BF16)
                    blocks.append(jnp.concatenate([values, zeros], 1))
                    blocks.append(jnp.concatenate([zeros, values], 1))
                weights.append(jnp.concatenate(blocks, 0))
            for pair in range(unroll):
                if window is None:
                    rows_in = left[...]
                else:
                    rows_in = left[pl.ds(pl.multiple_of(window * 256, 256), 256), :]
                product = dot_nt(rows_in, weights[pair]).astype(BF16)
                for ip in range(16 if window is None else 8):
                    quad = ip // 2 if window is None else window * 4 + ip // 2
                    for half in range(2):
                        at = pl.multiple_of((step * (2 * unroll) + pair * 2 + half) * 32, 32)
                        lanes = (ip % 2) * 128
                        piece = product[ip * 32 : (ip + 1) * 32, half * 128 : (half + 1) * 128]
                        if window is not None:
                            piece = piece + outer[quad, pl.ds(at, 32), lanes : lanes + 128]
                        outer[quad, pl.ds(at, 32), lanes : lanes + 128] = piece
            return inner

        lax.fori_loop(0, 16 // unroll, channels, 0)

    main_chain = chain_at[row_at * 32 + 16]
    one_chain(main_chain, None, 4)

    def more_chains(step, carry):
        chain = step + (step >= main_chain).astype(jnp.int32)
        one_chain(chain, (chain > main_chain).astype(jnp.int32), 2)
        return carry

    lax.fori_loop(first_chain, last_chain, more_chains, 0)

    eye = square_eye()
    bias = jnp.concatenate([bias_col[...], bias_col[...]], 1)
    scale_by = jnp.concatenate([gain_col[...], gain_col[...]], 1)

    def some_rows(step, carry):
        quads = [step * QUADS + q for q in range(QUADS)]
        mids = []
        for quad in quads:
            arriving = incoming[
                pl.ds(pl.multiple_of(quad * 4, 4), 4), pl.ds(pl.multiple_of(half_at * 64, 64), 64), :
            ].reshape(256, 128)
            mid = dot_nn(mixing[...], outer[quad]) + dot_nt(eye, arriving) + bias
            mids.append(mid.astype(BF16).astype(F32))
        normeds = []
        for mid in mids:
            center = jnp.sum(mid, axis=0, keepdims=True) * F32(1.0 / 128.0)
            shifted = mid - center
            spread = jnp.sum(shifted * shifted, axis=0, keepdims=True) * F32(1.0 / 128.0)
            normeds.append((shifted * lax.rsqrt(spread + F32(1e-05)) * scale_by).astype(BF16))
        results = list(mids)
        for part in range(2):
            for q in range(QUADS):
                gate = dot_nn(gate_up[part * 256 : (part + 1) * 256, :], normeds[q])
                up = dot_nn(gate_up[512 + part * 256 : 512 + (part + 1) * 256, :], normeds[q])
                half_gate = gate * F32(0.5)
                hidden = ((half_gate + half_gate * jnp.tanh(half_gate)) * up).astype(BF16)
                results[q] = results[q] + dot_nn(down[:, part * 256 : (part + 1) * 256], hidden)
        for q, quad in enumerate(quads):
            turned = turn(results[q].astype(BF16))
            out[pl.ds(pl.multiple_of(quad * 4, 4), 4)] = turned.astype(BF16).reshape(4, 64, 128)
            tile[pl.ds(pl.multiple_of(quad * 256, 256), 256), :] = turned
        return carry

    lax.fori_loop(0, 8 // QUADS, some_rows, 0)

    for group in range(8):
        for one in range(8):
            values = tile[pl.ds(group * 8 + one, 32, stride=64), :].astype(BF16)
            rows[group * 32 : (group + 1) * 32, one * 128 : (one + 1) * 128] = values
    sent[...] = dot_nt(rows[...], bins[...]).astype(BF16)
    keep[...] = sent[pl.ds(pl.multiple_of(core * 128, 128), 128), :]
    give[...] = sent[pl.ds(pl.multiple_of((1 - core) * 128, 128), 128), :]


def pair_call(meta, flip, chain_at, left_near, left_far, own, other, incoming, weights, so_far):
    by_half = pl.BlockSpec((32, 64, 128), lambda g, m, k: (0, half_of(m[0], flip), 0))
    operands = [left_near, left_far, own, other, chain_at.reshape(8, 128), incoming, *weights]
    operands = [in_vmem(values) for values in operands]
    specs = [VMEM_SPEC] * len(operands)
    aliases = {}
    if so_far is not None:
        operands.append(so_far)
        specs.append(pl.BlockSpec(memory_space=pl.ANY))
        aliases = {len(operands) + 1: 0}
    return pl.pallas_call(
        functools.partial(pair_kernel, flip=flip),
        out_shape=(
            jax.ShapeDtypeStruct((32, 128, 128), BF16),
            pltpu.VMEM((128, 512), BF16),
            pltpu.VMEM((128, 512), BF16),
        ),
        grid_spec=pltpu.PrefetchScalarGridSpec(
            num_scalar_prefetch=2,
            grid=(1,),
            in_specs=specs,
            out_specs=(by_half, VMEM_SPEC, VMEM_SPEC),
            scratch_shapes=[
                pltpu.VMEM((2048, 128), F32),
                pltpu.VMEM((512, 256), BF16),
                pltpu.VMEM((8, 1024, 256), BF16),
                pltpu.VMEM((2048, 128), F32),
                pltpu.VMEM((256, 1024), BF16),
                pltpu.VMEM((256, 512), BF16),
            ],
        ),
        input_output_aliases=aliases,
        compiler_params=pltpu.CompilerParams(vmem_limit_bytes=24 << 20),
        name="pair_half",
    )(meta, chain_at, *operands)


def own_kernel(tile, bins, bias, out):
    rows = pl.ds(pl.multiple_of(pl.program_id(0) * 8, 8), 8)
    flat_rows = jnp.concatenate([tile[i] for i in range(8)], axis=1)
    product = dot_nt(bins[...], flat_rows).astype(BF16).astype(F32)
    out[:, rows, :] = product.reshape(64, 8, 128) + bias[...][:, None, :]


def own_call(pair_out, bins, bias):
    return pl.pallas_call(
        own_kernel,
        out_shape=pltpu.VMEM((64, 32, 128), F32),
        grid=(4,),
        in_specs=[pl.BlockSpec((8, 128, 128), lambda g: (g, 0, 0)), VMEM_SPEC, VMEM_SPEC],
        out_specs=VMEM_SPEC,
        compiler_params=pltpu.CompilerParams(vmem_limit_bytes=16 << 20),
        name="own_bins",
    )(pair_out, in_vmem(bins), in_vmem(bias))


def join_kernel(meta, own, near, far, out, block):
    b_at = lax.rem(meta[0], 4)
    step = pl.program_id(0)
    rows = pl.ds(pl.multiple_of(step * 8, 8), 8)
    eye = square_eye()
    for source in range(4):
        from_b = jnp.bitwise_xor(b_at, source)
        at = pl.multiple_of(from_b * 32, 32)
        values = near if source < 2 else far
        block[pl.ds(at, 32), :] = values[source % 2, step]
    for part in range(4):
        turned = dot_nt(eye, block[:, part * 128 : (part + 1) * 128])
        out[part * 16 : (part + 1) * 16] = own[
            part * 16 : (part + 1) * 16, rows, :
        ] + turned.reshape(16, 8, 128)


def join_call(meta, own, near, far):
    return pl.pallas_call(
        join_kernel,
        out_shape=jax.ShapeDtypeStruct((64, 32, 128), F32),
        grid_spec=pltpu.PrefetchScalarGridSpec(
            num_scalar_prefetch=1,
            grid=(4,),
            in_specs=[VMEM_SPEC, VMEM_SPEC, VMEM_SPEC],
            out_specs=pl.BlockSpec((64, 8, 128), lambda g, m: (0, g, 0)),
            scratch_shapes=[pltpu.VMEM((128, 512), BF16)],
        ),
        compiler_params=pltpu.CompilerParams(vmem_limit_bytes=16 << 20),
        name="join_bins",
    )(meta, in_vmem(own), in_vmem(near), in_vmem(far))


def per_device(
    first_homolog_embedding,
    second_homolog_embedding,
    token_chain_index,
    incoming_pair_state,
    tensor_mixing_matrix,
    outer_product_bias,
    transition_norm_gain,
    transition_gate_weight,
    transition_up_weight,
    transition_down_weight,
    distogram_weight,
    distogram_bias,
):
    row_at = lax.axis_index("row").astype(jnp.int32)
    col_at = lax.axis_index("col").astype(jnp.int32)
    meta = jnp.stack([row_at, col_at])

    left = jnp.transpose(first_homolog_embedding, (1, 2, 0)).reshape(1, 128, 128)
    right = jnp.transpose(second_homolog_embedding, (1, 2, 0)).reshape(1, 128, 128)

    centre = send(right, lambda a, b, c: (c, b, a))
    *weights, bin_col = prep_call(
        tensor_mixing_matrix,
        transition_gate_weight,
        transition_up_weight,
        transition_down_weight,
        distogram_weight,
        outer_product_bias,
        transition_norm_gain,
        distogram_bias,
    )
    left_two = jnp.concatenate([left, send(left, lambda a, b, c: (a, b, c ^ 1))], 0)
    before = send(centre, lambda a, b, c: ((a + 1) % 8, b, c))
    after = send(centre, lambda a, b, c: ((a - 1) % 8, b, c))
    left_near = jnp.concatenate([left_two, send(left_two, lambda a, b, c: (a, b, c ^ 4))], 0)
    three = jnp.concatenate([before, centre, after], 0)
    low = send(three, lambda a, b, c: ((a + 3) % 8, b, c))
    high = send(three[:2], lambda a, b, c: ((a - 3) % 8, b, c))
    left_far = send(left_near, lambda a, b, c: (a, b, c ^ 2))
    own = jnp.concatenate([low, three, high], 0)
    other = send(own, lambda a, b, c: (a, b ^ 1, c))
    own_far = send(own, lambda a, b, c: (a, b ^ 2, c))

    pair_out, keep, give = pair_call(
        meta, False, token_chain_index, left_near, left_far, own, other,
        incoming_pair_state, weights, None,
    )
    other_far = send(own_far, lambda a, b, c: (a, b ^ 1, c))
    given = send(give, lambda a, b, c: (a, b ^ 1, c))
    near = send(jnp.stack([keep, given]), lambda a, b, c: (c, b, a))
    pair_out, keep, give = pair_call(
        meta, True, token_chain_index, left_near, left_far, own_far, other_far,
        incoming_pair_state, weights, pair_out,
    )
    given = send(give, lambda a, b, c: (a, b ^ 1, c))
    far = send(jnp.stack([keep, given]), lambda a, b, c: (c, b ^ 2, a))

    own_bins = own_call(pair_out, weights[3], bin_col)
    logits = join_call(
        meta, own_bins, near.reshape(2, 4, 32, 512), far.reshape(2, 4, 32, 512)
    )
    return (pair_out, logits)


def solution(mesh):
    placed = (
        P(None, ("row", "col"), None),
        P(None, ("row", "col"), None),
        P(),
        P("row", "col", None),
        P(),
        P(),
        P(),
        P(),
        P(),
        P(),
        P(),
        P(),
    )
    return jax.shard_map(
        per_device,
        mesh=mesh,
        in_specs=placed,
        out_specs=(P("row", "col", None), P(None, "row", "col")),
        check_vma=False,
    )
```

```python
import functools

import jax
import jax.numpy as jnp
from jax import lax
from jax.experimental import pallas as pl
from jax.experimental.pallas import tpu as pltpu
from jax.sharding import PartitionSpec as P


AXES = ("row", "col")
F32 = jnp.float32
BF16 = jnp.bfloat16
DEVICES = [(a, b, c) for a in range(8) for b in range(4) for c in range(8)]
COL_MASKS = (0, 1, 4, 5, 2, 3, 6, 7)
QUADS = 2


def in_vmem(values):
    return pltpu.with_memory_space_constraint(values, pltpu.VMEM)


VMEM_SPEC = pl.BlockSpec(memory_space=pltpu.VMEM)


def flat(a, b, c):
    return (a * 4 + b) * 8 + c


def send(values, target):
    pairs = [(flat(*here), flat(*target(*here))) for here in DEVICES]
    return lax.ppermute(values, AXES, pairs)


def dot_nt(left, right):
    return lax.dot_general(left, right, (((1,), (1,)), ((), ())), preferred_element_type=F32)


def dot_nn(left, right):
    return lax.dot_general(left, right, (((1,), (0,)), ((), ())), preferred_element_type=F32)


def square_eye():
    down = lax.broadcasted_iota(jnp.int32, (128, 128), 0)
    along = lax.broadcasted_iota(jnp.int32, (128, 128), 1)
    return (down == along).astype(F32).astype(BF16)


def turn(values):
    return jnp.transpose(values.astype(F32), (1, 0))


def prep_kernel(
    mix, gate, up, down_w, bins_w, outer_bias, gain, bin_bias,
    mixing, gate_up, down, bins, bias_col, gain_col, bin_col, wide,
):
    wide[...] = mix[...].astype(F32)
    for block in range(8):
        parts = [wide[pl.ds(block * 4 + d, 32, stride=32), :] for d in range(4)]
        mixing[:, block * 128 : (block + 1) * 128] = turn(jnp.concatenate(parts, 0)).astype(BF16)
    for block in range(4):
        lanes = slice(block * 128, (block + 1) * 128)
        gate_up[block * 128 : (block + 1) * 128, :] = turn(gate[:, lanes]).astype(BF16)
        gate_up[512 + block * 128 : 512 + (block + 1) * 128, :] = turn(up[:, lanes]).astype(BF16)
        down[:, lanes] = turn(down_w[lanes, :]).astype(BF16)
    spread = jnp.broadcast_to(bins_w[...].astype(F32)[:, None, :], (64, 8, 128)).reshape(512, 128)
    which = lax.rem(lax.broadcasted_iota(jnp.int32, (512, 128), 0), 8)
    for one in range(8):
        bins[:, one * 128 : (one + 1) * 128] = jnp.where(which == one, spread, 0.0).astype(BF16)
    bias_col[...] = turn(jnp.broadcast_to(outer_bias[...], (128, 128)))
    gain_col[...] = turn(jnp.broadcast_to(gain[...], (128, 128)))
    bin_col[...] = turn(jnp.broadcast_to(bin_bias[...], (128, 64)))


def prep_call(mix, gate, up, down, bins, outer_bias, gain, bin_bias):
    operands = (mix, gate, up, down, bins.T, outer_bias[None], gain[None], bin_bias[None])
    return pl.pallas_call(
        prep_kernel,
        out_shape=(
            pltpu.VMEM((128, 1024), BF16),
            pltpu.VMEM((1024, 128), BF16),
            pltpu.VMEM((128, 512), BF16),
            pltpu.VMEM((512, 1024), BF16),
            pltpu.VMEM((128, 128), F32),
            pltpu.VMEM((128, 128), F32),
            pltpu.VMEM((64, 128), F32),
        ),
        out_specs=[VMEM_SPEC] * 7,
        scratch_shapes=[pltpu.VMEM((1024, 128), F32)],
        compiler_params=pltpu.CompilerParams(vmem_limit_bytes=16 << 20),
        name="prep",
    )(*[pltpu.with_memory_space_constraint(v, pltpu.HBM) for v in operands])


def half_of(row_at, flip):
    x_lo = lax.rem(lax.div(row_at, 2), 2)
    return 1 - x_lo if flip else x_lo


def outer_kernel(
    meta,
    chain_at,
    left_near,
    left_far,
    right_own,
    right_other,
    chains,
    outer,
    right,
    left,
    *,
    flip,
):
    row_at, col_at = meta[0], meta[1]
    half_at = half_of(row_at, flip)
    z_at = lax.div(row_at, 4)
    core = lax.rem(row_at, 2)
    first_chain = chain_at[row_at * 32]
    last_chain = chain_at[row_at * 32 + 31]

    for step in range(8):
        place = lax.rem(z_at + (step + 4), 8)
        own_row = pl.multiple_of((core * 8 + place) * 128, 128)
        other_row = pl.multiple_of(((1 - core) * 8 + place) * 128, 128)
        right[pl.ds(own_row, 128), :] = right_own[step].astype(F32)
        right[pl.ds(other_row, 128), :] = right_other[step].astype(F32)

    paired = lax.broadcasted_iota(jnp.int32, (64, 128), 1) < 64
    token = lax.broadcasted_iota(jnp.int32, (64, 128), 0) + (col_at * 128 + half_at * 64)
    zeros = jnp.zeros((64, 128), BF16)

    def one_chain(chain, window, unroll):
        for step, mask in enumerate(COL_MASKS):
            place = jnp.bitwise_xor(col_at, mask)
            chunk = left_near[step] if step < 4 else left_far[step - 4]
            for t in range(4):
                of_row = chain_at[row_at * 32 + place * 4 + t]
                values = chunk[t * 32 : (t + 1) * 32, :]
                values = jnp.where(of_row == chain, values, jnp.zeros_like(values))
                at = pl.multiple_of((place * 2 + t // 2) * 32, 32)
                left[pl.ds(at, 32), (t % 2) * 128 : (t % 2) * 128 + 128] = values
        start = jnp.sum((chains[...] < chain).astype(F32)).astype(jnp.int32)
        stop = jnp.sum((chains[...] <= chain).astype(F32)).astype(jnp.int32)
        same = jnp.logical_and(token >= start, token < stop)
        scale = jnp.where(
            same,
            F32(1.0 / 128.0),
            jnp.where(paired, F32(1.0 / 64.0), F32(0.0)),
        )

        def channels(step, inner):
            weights = []
            for pair in range(unroll):
                blocks = []
                for half in range(2):
                    d = step * (2 * unroll) + pair * 2 + half
                    values = (right[pl.ds(d, 64, stride=32), :] * scale).astype(BF16)
                    blocks.append(jnp.concatenate([values, zeros], 1))
                    blocks.append(jnp.concatenate([zeros, values], 1))
                weights.append(jnp.concatenate(blocks, 0))
            for pair in range(unroll):
                if window is None:
                    rows_in = left[...]
                else:
                    rows_in = left[pl.ds(pl.multiple_of(window * 256, 256), 256), :]
                product = dot_nt(rows_in, weights[pair]).astype(BF16)
                for ip in range(16 if window is None else 8):
                    quad = ip // 2 if window is None else window * 4 + ip // 2
                    for half in range(2):
                        at = pl.multiple_of((step * (2 * unroll) + pair * 2 + half) * 32, 32)
                        lanes = (ip % 2) * 128
                        piece = product[ip * 32 : (ip + 1) * 32, half * 128 : (half + 1) * 128]
                        if window is not None:
                            piece = piece + outer[quad, pl.ds(at, 32), lanes : lanes + 128]
                        outer[quad, pl.ds(at, 32), lanes : lanes + 128] = piece
            return inner

        lax.fori_loop(0, 16 // unroll, channels, 0)

    main_chain = chain_at[row_at * 32 + 16]
    one_chain(main_chain, None, 4)

    def more_chains(step, carry):
        chain = step + (step >= main_chain).astype(jnp.int32)
        one_chain(chain, (chain > main_chain).astype(jnp.int32), 2)
        return carry

    lax.fori_loop(first_chain, last_chain, more_chains, 0)


def outer_call(meta, flip, chain_at, left_near, left_far, own, other):
    operands = [left_near, left_far, own, other, chain_at.reshape(8, 128)]
    return pl.pallas_call(
        functools.partial(outer_kernel, flip=flip),
        out_shape=pltpu.VMEM((8, 1024, 256), BF16),
        grid_spec=pltpu.PrefetchScalarGridSpec(
            num_scalar_prefetch=2,
            grid=(1,),
            in_specs=[VMEM_SPEC] * len(operands),
            out_specs=VMEM_SPEC,
            scratch_shapes=[pltpu.VMEM((2048, 128), F32), pltpu.VMEM((512, 256), BF16)],
        ),
        compiler_params=pltpu.CompilerParams(vmem_limit_bytes=12 << 20),
        name="outer_half",
    )(meta, chain_at, *[in_vmem(values) for values in operands])


def rows_kernel(
    meta, outer, incoming, mixing, gate_up, down, bins, bias_col, gain_col, *rest, flip, part_at
):
    out, sent, tile, rows = rest[-4:]
    row_at = meta[0]
    core = lax.rem(row_at, 2)
    half_at = half_of(row_at, flip)
    eye = square_eye()
    bias = jnp.concatenate([bias_col[...], bias_col[...]], 1)
    scale_by = jnp.concatenate([gain_col[...], gain_col[...]], 1)

    def some_rows(step, carry):
        quads = [step * QUADS + q for q in range(QUADS)]
        mids = []
        for quad in quads:
            arriving = incoming[
                pl.ds(pl.multiple_of(part_at * 16 + quad * 4, 4), 4),
                pl.ds(pl.multiple_of(half_at * 64, 64), 64),
                :,
            ].reshape(256, 128)
            mid = dot_nn(mixing[...], outer[part_at * 4 + quad]) + dot_nt(eye, arriving) + bias
            mids.append(mid.astype(BF16).astype(F32))
        normeds = []
        for mid in mids:
            center = jnp.sum(mid, axis=0, keepdims=True) * F32(1.0 / 128.0)
            shifted = mid - center
            spread = jnp.sum(shifted * shifted, axis=0, keepdims=True) * F32(1.0 / 128.0)
            normeds.append((shifted * lax.rsqrt(spread + F32(1e-05)) * scale_by).astype(BF16))
        results = list(mids)
        for part in range(2):
            for q in range(QUADS):
                gate = dot_nn(gate_up[part * 256 : (part + 1) * 256, :], normeds[q])
                up = dot_nn(gate_up[512 + part * 256 : 512 + (part + 1) * 256, :], normeds[q])
                half_gate = gate * F32(0.5)
                hidden = ((half_gate + half_gate * jnp.tanh(half_gate)) * up).astype(BF16)
                results[q] = results[q] + dot_nn(down[:, part * 256 : (part + 1) * 256], hidden)
        for q, quad in enumerate(quads):
            turned = turn(results[q].astype(BF16))
            out[pl.ds(pl.multiple_of(quad * 4, 4), 4)] = turned.astype(BF16).reshape(4, 64, 128)
            tile[pl.ds(pl.multiple_of(quad * 256, 256), 256), :] = turned
        return carry

    lax.fori_loop(0, 4 // QUADS, some_rows, 0)

    for group in range(8):
        for one in range(8):
            values = tile[pl.ds(group * 8 + one, 16, stride=64), :].astype(BF16)
            rows[group * 16 : (group + 1) * 16, one * 128 : (one + 1) * 128] = values
    product = dot_nt(rows[...], bins[...]).astype(BF16).reshape(2, 4, 16, 512)
    sent[core] = product[0]
    sent[1 - core] = product[1]


def rows_call(meta, flip, part_at, outer, incoming, weights, so_far):
    block = pl.BlockSpec((16, 64, 128), lambda g, m: (part_at, half_of(m[0], flip), 0))
    operands = [in_vmem(values) for values in (outer, incoming, *weights)]
    specs = [VMEM_SPEC] * len(operands)
    aliases = {}
    if so_far is not None:
        operands.append(so_far)
        specs.append(pl.BlockSpec(memory_space=pl.ANY))
        aliases = {len(operands): 0}
    return pl.pallas_call(
        functools.partial(rows_kernel, flip=flip, part_at=part_at),
        out_shape=(
            jax.ShapeDtypeStruct((32, 128, 128), BF16),
            pltpu.VMEM((2, 4, 16, 512), BF16),
        ),
        grid_spec=pltpu.PrefetchScalarGridSpec(
            num_scalar_prefetch=1,
            grid=(1,),
            in_specs=specs,
            out_specs=(block, VMEM_SPEC),
            scratch_shapes=[pltpu.VMEM((1024, 128), F32), pltpu.VMEM((128, 1024), BF16)],
        ),
        input_output_aliases=aliases,
        compiler_params=pltpu.CompilerParams(vmem_limit_bytes=12 << 20),
        name="rows_part",
    )(meta, *operands)


def own_kernel(tile, bins, bias, out):
    rows = pl.ds(pl.multiple_of(pl.program_id(0) * 8, 8), 8)
    flat_rows = jnp.concatenate([tile[i] for i in range(8)], axis=1)
    product = dot_nt(bins[...], flat_rows).astype(BF16).astype(F32)
    out[:, rows, :] = product.reshape(64, 8, 128) + bias[...][:, None, :]


def own_call(pair_out, bins, bias):
    return pl.pallas_call(
        own_kernel,
        out_shape=pltpu.VMEM((64, 32, 128), F32),
        grid=(4,),
        in_specs=[pl.BlockSpec((8, 128, 128), lambda g: (g, 0, 0)), VMEM_SPEC, VMEM_SPEC],
        out_specs=VMEM_SPEC,
        compiler_params=pltpu.CompilerParams(vmem_limit_bytes=16 << 20),
        name="own_bins",
    )(pair_out, in_vmem(bins), in_vmem(bias))


def join_kernel(meta, own, *rest):
    out, block = rest[-2:]
    b_at = lax.rem(meta[0], 4)
    step = pl.program_id(0)
    rows = pl.ds(pl.multiple_of(step * 8, 8), 8)
    eye = square_eye()
    for piece in range(4):
        mine, partner = rest[piece * 2], rest[piece * 2 + 1]
        for side, values in enumerate((mine, partner)):
            from_b = jnp.bitwise_xor(b_at, (piece // 2) * 2 + side)
            at = pl.multiple_of(from_b * 32 + (piece % 2) * 16, 16)
            block[pl.ds(at, 16), :] = values[side, step]
    for part in range(4):
        turned = dot_nt(eye, block[:, part * 128 : (part + 1) * 128])
        out[part * 16 : (part + 1) * 16] = own[
            part * 16 : (part + 1) * 16, rows, :
        ] + turned.reshape(16, 8, 128)


def join_call(meta, own, pieces):
    return pl.pallas_call(
        join_kernel,
        out_shape=jax.ShapeDtypeStruct((64, 32, 128), F32),
        grid_spec=pltpu.PrefetchScalarGridSpec(
            num_scalar_prefetch=1,
            grid=(4,),
            in_specs=[VMEM_SPEC] * 9,
            out_specs=pl.BlockSpec((64, 8, 128), lambda g, m: (0, g, 0)),
            scratch_shapes=[pltpu.VMEM((128, 512), BF16)],
        ),
        compiler_params=pltpu.CompilerParams(vmem_limit_bytes=16 << 20),
        name="join_bins",
    )(meta, in_vmem(own), *[in_vmem(values) for values in pieces])


def per_device(
    first_homolog_embedding,
    second_homolog_embedding,
    token_chain_index,
    incoming_pair_state,
    tensor_mixing_matrix,
    outer_product_bias,
    transition_norm_gain,
    transition_gate_weight,
    transition_up_weight,
    transition_down_weight,
    distogram_weight,
    distogram_bias,
):
    row_at = lax.axis_index("row").astype(jnp.int32)
    col_at = lax.axis_index("col").astype(jnp.int32)
    meta = jnp.stack([row_at, col_at])

    left = jnp.transpose(first_homolog_embedding, (1, 2, 0)).reshape(1, 128, 128)
    right = jnp.transpose(second_homolog_embedding, (1, 2, 0)).reshape(1, 128, 128)

    centre = send(right, lambda a, b, c: (c, b, a))
    *weights, bin_col = prep_call(
        tensor_mixing_matrix,
        transition_gate_weight,
        transition_up_weight,
        transition_down_weight,
        distogram_weight,
        outer_product_bias,
        transition_norm_gain,
        distogram_bias,
    )
    left_two = jnp.concatenate([left, send(left, lambda a, b, c: (a, b, c ^ 1))], 0)
    before = send(centre, lambda a, b, c: ((a + 1) % 8, b, c))
    after = send(centre, lambda a, b, c: ((a - 1) % 8, b, c))
    left_near = jnp.concatenate([left_two, send(left_two, lambda a, b, c: (a, b, c ^ 4))], 0)
    three = jnp.concatenate([before, centre, after], 0)
    low = send(three, lambda a, b, c: ((a + 3) % 8, b, c))
    high = send(three[:2], lambda a, b, c: ((a - 3) % 8, b, c))
    left_far = send(left_near, lambda a, b, c: (a, b, c ^ 2))
    own = jnp.concatenate([low, three, high], 0)
    other = send(own, lambda a, b, c: (a, b ^ 1, c))
    own_far = send(own, lambda a, b, c: (a, b ^ 2, c))

    pieces = []
    pair_out = None
    for flip in (False, True):
        if flip:
            other = send(own_far, lambda a, b, c: (a, b ^ 1, c))
            own = own_far
        outer = outer_call(meta, flip, token_chain_index, left_near, left_far, own, other)
        for part_at in range(2):
            pair_out, sent = rows_call(
                meta, flip, part_at, outer, incoming_pair_state, weights, pair_out
            )
            pieces.append(send(sent, lambda a, b, c, x=2 * flip: (c, b ^ x, a)))
    arrived = []
    for piece in pieces:
        arrived += [piece, send(piece, lambda a, b, c: (a, b ^ 1, c))]

    own_bins = own_call(pair_out, weights[3], bin_col)
    logits = join_call(meta, own_bins, arrived)
    return (pair_out, logits)


def solution(mesh):
    placed = (
        P(None, ("row", "col"), None),
        P(None, ("row", "col"), None),
        P(),
        P("row", "col", None),
        P(),
        P(),
        P(),
        P(),
        P(),
        P(),
        P(),
        P(),
    )
    return jax.shard_map(
        per_device,
        mesh=mesh,
        in_specs=placed,
        out_specs=(P("row", "col", None), P(None, "row", "col")),
        check_vma=False,
    )
```

```python
import functools

import jax
import jax.numpy as jnp
from jax import lax
from jax.experimental import pallas as pl
from jax.experimental.pallas import tpu as pltpu
from jax.sharding import PartitionSpec as P


AXES = ("row", "col")
F32 = jnp.float32
BF16 = jnp.bfloat16
DEVICES = [(a, b, c) for a in range(8) for b in range(4) for c in range(8)]
COL_MASKS = (0, 1, 4, 5, 2, 3, 6, 7)


def in_vmem(values):
    return pltpu.with_memory_space_constraint(values, pltpu.VMEM)


VMEM_SPEC = pl.BlockSpec(memory_space=pltpu.VMEM)


def flat(a, b, c):
    return (a * 4 + b) * 8 + c


def send(values, target):
    pairs = [(flat(*here), flat(*target(*here))) for here in DEVICES]
    return lax.ppermute(values, AXES, pairs)


def dot_nt(left, right):
    return lax.dot_general(left, right, (((1,), (1,)), ((), ())), preferred_element_type=F32)


def dot_nn(left, right):
    return lax.dot_general(left, right, (((1,), (0,)), ((), ())), preferred_element_type=F32)


def square_eye():
    down = lax.broadcasted_iota(jnp.int32, (128, 128), 0)
    along = lax.broadcasted_iota(jnp.int32, (128, 128), 1)
    return (down == along).astype(F32).astype(BF16)


def turn(values):
    return jnp.transpose(values.astype(F32), (1, 0))


def prep_kernel(
    mix, gate, up, down_w, bins_w, outer_bias, gain, bin_bias, chain_in,
    mixing, gate_up, down, bins, bias_col, gain_col, bin_col, chains, wide,
):
    chains[...] = chain_in[...]
    wide[...] = mix[...].astype(F32)
    for block in range(8):
        parts = [wide[pl.ds(block * 4 + d, 32, stride=32), :] for d in range(4)]
        mixing[:, block * 128 : (block + 1) * 128] = turn(jnp.concatenate(parts, 0)).astype(BF16)
    for block in range(4):
        lanes = slice(block * 128, (block + 1) * 128)
        gate_up[block * 128 : (block + 1) * 128, :] = turn(gate[:, lanes]).astype(BF16)
        gate_up[512 + block * 128 : 512 + (block + 1) * 128, :] = turn(up[:, lanes]).astype(BF16)
        down[:, lanes] = turn(down_w[lanes, :]).astype(BF16)
    spread = jnp.broadcast_to(bins_w[...].astype(F32)[:, None, :], (64, 8, 128)).reshape(512, 128)
    which = lax.rem(lax.broadcasted_iota(jnp.int32, (512, 128), 0), 8)
    for one in range(8):
        bins[:, one * 128 : (one + 1) * 128] = jnp.where(which == one, spread, 0.0).astype(BF16)
    bias_col[...] = turn(jnp.broadcast_to(outer_bias[...], (128, 128)))
    gain_col[...] = turn(jnp.broadcast_to(gain[...], (128, 128)))
    bin_col[...] = turn(jnp.broadcast_to(bin_bias[...], (128, 64)))


def prep_call(mix, gate, up, down, bins, outer_bias, gain, bin_bias, chain_at):
    operands = (mix, gate, up, down, bins.T, outer_bias[None], gain[None], bin_bias[None])
    operands += (chain_at.reshape(8, 128),)
    return pl.pallas_call(
        prep_kernel,
        out_shape=(
            pltpu.VMEM((128, 1024), BF16),
            pltpu.VMEM((1024, 128), BF16),
            pltpu.VMEM((128, 512), BF16),
            pltpu.VMEM((512, 1024), BF16),
            pltpu.VMEM((128, 128), F32),
            pltpu.VMEM((128, 128), F32),
            pltpu.VMEM((64, 128), F32),
            pltpu.VMEM((8, 128), jnp.int32),
        ),
        out_specs=[VMEM_SPEC] * 8,
        scratch_shapes=[pltpu.VMEM((1024, 128), F32)],
        compiler_params=pltpu.CompilerParams(vmem_limit_bytes=16 << 20),
        name="prep",
    )(*[pltpu.with_memory_space_constraint(v, pltpu.HBM) for v in operands])


def half_of(row_at, flip):
    x_lo = lax.rem(lax.div(row_at, 2), 2)
    return 1 - x_lo if flip else x_lo


def outer_kernel(
    meta,
    chain_at,
    left_near,
    left_far,
    right_own,
    right_other,
    chains,
    outer,
    right,
    left,
    packed,
    *,
    flip,
):
    row_at, col_at = meta[0], meta[1]
    half_at = half_of(row_at, flip)
    z_at = lax.div(row_at, 4)
    core = lax.rem(row_at, 2)
    first_chain = chain_at[row_at * 32]
    last_chain = chain_at[row_at * 32 + 31]

    for step in range(8):
        place = lax.rem(z_at + (step + 4), 8)
        own_row = pl.multiple_of((core * 8 + place) * 128, 128)
        other_row = pl.multiple_of(((1 - core) * 8 + place) * 128, 128)
        right[pl.ds(own_row, 128), :] = right_own[step].astype(F32)
        right[pl.ds(other_row, 128), :] = right_other[step].astype(F32)

    paired = lax.broadcasted_iota(jnp.int32, (64, 128), 1) < 64
    token = lax.broadcasted_iota(jnp.int32, (64, 128), 0) + (col_at * 128 + half_at * 64)
    zeros = jnp.zeros((64, 128), BF16)

    def one_chain(chain, window, unroll):
        for step, mask in enumerate(COL_MASKS):
            place = jnp.bitwise_xor(col_at, mask)
            chunk = left_near[step] if step < 4 else left_far[step - 4]
            for t in range(4):
                of_row = chain_at[row_at * 32 + place * 4 + t]
                values = chunk[t * 32 : (t + 1) * 32, :]
                values = jnp.where(of_row == chain, values, jnp.zeros_like(values))
                at = pl.multiple_of((place * 2 + t // 2) * 32, 32)
                left[pl.ds(at, 32), (t % 2) * 128 : (t % 2) * 128 + 128] = values
        start = jnp.sum((chains[...] < chain).astype(F32)).astype(jnp.int32)
        stop = jnp.sum((chains[...] <= chain).astype(F32)).astype(jnp.int32)
        same = jnp.logical_and(token >= start, token < stop)
        scale = jnp.where(
            same,
            F32(1.0 / 128.0),
            jnp.where(paired, F32(1.0 / 64.0), F32(0.0)),
        ).astype(BF16)

        def channels(step, inner):
            weights = []
            for pair in range(unroll):
                blocks = []
                for half in range(2):
                    d = step * (2 * unroll) + pair * 2 + half
                    at = pl.multiple_of(d * 64, 64)
                    if window is None:
                        values = right[pl.ds(d, 64, stride=32), :].astype(BF16)
                        packed[pl.ds(at, 64), :] = values
                    else:
                        values = packed[pl.ds(at, 64), :]
                    values = values * scale
                    blocks.append(jnp.concatenate([values, zeros], 1))
                    blocks.append(jnp.concatenate([zeros, values], 1))
                weights.append(jnp.concatenate(blocks, 0))
            for pair in range(unroll):
                if window is None:
                    rows_in = left[...]
                else:
                    rows_in = left[pl.ds(pl.multiple_of(window * 256, 256), 256), :]
                product = dot_nt(rows_in, weights[pair]).astype(BF16)
                for ip in range(16 if window is None else 8):
                    quad = ip // 2 if window is None else window * 4 + ip // 2
                    for half in range(2):
                        at = pl.multiple_of((step * (2 * unroll) + pair * 2 + half) * 32, 32)
                        lanes = (ip % 2) * 128
                        piece = product[ip * 32 : (ip + 1) * 32, half * 128 : (half + 1) * 128]
                        if window is not None:
                            piece = piece + outer[quad, pl.ds(at, 32), lanes : lanes + 128]
                        outer[quad, pl.ds(at, 32), lanes : lanes + 128] = piece
            return inner

        lax.fori_loop(0, 16 // unroll, channels, 0)

    main_chain = chain_at[row_at * 32 + 16]
    one_chain(main_chain, None, 4)

    def more_chains(step, carry):
        chain = step + (step >= main_chain).astype(jnp.int32)
        one_chain(chain, (chain > main_chain).astype(jnp.int32), 4)
        return carry

    lax.fori_loop(first_chain, last_chain, more_chains, 0)


def outer_call(meta, flip, chain_at, chains, left_near, left_far, own, other):
    operands = [left_near, left_far, own, other, chains]
    return pl.pallas_call(
        functools.partial(outer_kernel, flip=flip),
        out_shape=pltpu.VMEM((8, 1024, 256), BF16),
        grid_spec=pltpu.PrefetchScalarGridSpec(
            num_scalar_prefetch=2,
            grid=(1,),
            in_specs=[VMEM_SPEC] * len(operands),
            out_specs=VMEM_SPEC,
            scratch_shapes=[
                pltpu.VMEM((2048, 128), F32),
                pltpu.VMEM((512, 256), BF16),
                pltpu.VMEM((2048, 128), BF16),
            ],
        ),
        compiler_params=pltpu.CompilerParams(vmem_limit_bytes=12 << 20),
        name="outer_half",
    )(
        meta,
        pltpu.with_memory_space_constraint(chain_at, pltpu.HBM),
        *[in_vmem(values) for values in operands],
    )


def rows_kernel(
    meta, outer, incoming, mixing, gate_up, down, bins, bias_col, gain_col, *rest, flip, part_at
):
    out, sent, tile, rows = rest[-4:]
    row_at = meta[0]
    core = lax.rem(row_at, 2)
    half_at = half_of(row_at, flip)
    eye = square_eye()
    bias = jnp.concatenate([bias_col[...], bias_col[...]], 1)
    scale_by = jnp.concatenate([gain_col[...], gain_col[...]], 1)

    def mixed(quad):
        arriving = incoming[
            pl.ds(pl.multiple_of(part_at * 16 + quad * 4, 4), 4),
            pl.ds(pl.multiple_of(half_at * 64, 64), 64),
            :,
        ].reshape(256, 128)
        mid = dot_nn(mixing[...], outer[part_at * 4 + quad]) + dot_nt(eye, arriving) + bias
        return mid.astype(BF16).astype(F32)

    def normalised(mid):
        center = jnp.sum(mid, axis=0, keepdims=True) * F32(1.0 / 128.0)
        shifted = mid - center
        spread = jnp.sum(shifted * shifted, axis=0, keepdims=True) * F32(1.0 / 128.0)
        return (shifted * lax.rsqrt(spread + F32(1e-05)) * scale_by).astype(BF16)

    def widened(normed, part):
        gate = dot_nn(gate_up[part * 256 : (part + 1) * 256, :], normed)
        up = dot_nn(gate_up[512 + part * 256 : 512 + (part + 1) * 256, :], normed)
        half_gate = gate * F32(0.5)
        return ((half_gate + half_gate * jnp.tanh(half_gate)) * up).astype(BF16)

    def narrowed(hidden, part):
        return dot_nn(down[:, part * 256 : (part + 1) * 256], hidden)

    def finish(quad, result):
        turned = turn(result.astype(BF16))
        out[quad * 4 : quad * 4 + 4] = turned.astype(BF16).reshape(4, 64, 128)
        tile[quad * 256 : (quad + 1) * 256, :] = turned

    mid = mixed(0)
    normed = normalised(mid)
    for quad in range(4):
        following = mixed(quad + 1) if quad + 1 < 4 else None
        result = mid
        hidden = widened(normed, 0)
        for part in range(1, 2):
            ahead = widened(normed, part)
            result = result + narrowed(hidden, part - 1)
            hidden = ahead
        if following is not None:
            normed = normalised(following)
        result = result + narrowed(hidden, 1)
        finish(quad, result)
        mid = following

    for group in range(8):
        for one in range(8):
            values = tile[pl.ds(group * 8 + one, 16, stride=64), :].astype(BF16)
            rows[group * 16 : (group + 1) * 16, one * 128 : (one + 1) * 128] = values
    product = dot_nt(rows[...], bins[...]).astype(BF16).reshape(2, 4, 16, 512)
    sent[core] = product[0]
    sent[1 - core] = product[1]


def rows_call(meta, flip, part_at, outer, incoming, weights, so_far):
    block = pl.BlockSpec((16, 64, 128), lambda g, m: (part_at, half_of(m[0], flip), 0))
    operands = [in_vmem(values) for values in (outer, incoming, *weights)]
    specs = [VMEM_SPEC] * len(operands)
    aliases = {}
    if so_far is not None:
        operands.append(so_far)
        specs.append(pl.BlockSpec(memory_space=pl.ANY))
        aliases = {len(operands): 0}
    return pl.pallas_call(
        functools.partial(rows_kernel, flip=flip, part_at=part_at),
        out_shape=(
            jax.ShapeDtypeStruct((32, 128, 128), BF16),
            pltpu.VMEM((2, 4, 16, 512), BF16),
        ),
        grid_spec=pltpu.PrefetchScalarGridSpec(
            num_scalar_prefetch=1,
            grid=(1,),
            in_specs=specs,
            out_specs=(block, VMEM_SPEC),
            scratch_shapes=[pltpu.VMEM((1024, 128), F32), pltpu.VMEM((128, 1024), BF16)],
        ),
        input_output_aliases=aliases,
        compiler_params=pltpu.CompilerParams(vmem_limit_bytes=12 << 20),
        name="rows_part",
    )(meta, *operands)


def own_kernel(tile, bins, bias, out):
    rows = pl.ds(pl.multiple_of(pl.program_id(0) * 8, 8), 8)
    flat_rows = jnp.concatenate([tile[i] for i in range(8)], axis=1)
    product = dot_nt(bins[...], flat_rows).astype(BF16).astype(F32)
    out[:, rows, :] = product.reshape(64, 8, 128) + bias[...][:, None, :]


def own_call(pair_out, bins, bias):
    return pl.pallas_call(
        own_kernel,
        out_shape=pltpu.VMEM((64, 32, 128), F32),
        grid=(4,),
        in_specs=[pl.BlockSpec((8, 128, 128), lambda g: (g, 0, 0)), VMEM_SPEC, VMEM_SPEC],
        out_specs=VMEM_SPEC,
        compiler_params=pltpu.CompilerParams(vmem_limit_bytes=16 << 20),
        name="own_bins",
    )(pair_out, in_vmem(bins), in_vmem(bias))


def join_kernel(meta, own, *rest):
    out, block = rest[-2:]
    b_at = lax.rem(meta[0], 4)
    step = pl.program_id(0)
    rows = pl.ds(pl.multiple_of(step * 8, 8), 8)
    eye = square_eye()
    for piece in range(4):
        mine, partner = rest[piece * 2], rest[piece * 2 + 1]
        for side, values in enumerate((mine, partner)):
            from_b = jnp.bitwise_xor(b_at, (piece // 2) * 2 + side)
            at = pl.multiple_of(from_b * 32 + (piece % 2) * 16, 16)
            block[pl.ds(at, 16), :] = values[side, step]
    for part in range(4):
        turned = dot_nt(eye, block[:, part * 128 : (part + 1) * 128])
        out[part * 16 : (part + 1) * 16] = own[
            part * 16 : (part + 1) * 16, rows, :
        ] + turned.reshape(16, 8, 128)


def join_call(meta, own, pieces):
    return pl.pallas_call(
        join_kernel,
        out_shape=jax.ShapeDtypeStruct((64, 32, 128), F32),
        grid_spec=pltpu.PrefetchScalarGridSpec(
            num_scalar_prefetch=1,
            grid=(4,),
            in_specs=[VMEM_SPEC] * 9,
            out_specs=pl.BlockSpec((64, 8, 128), lambda g, m: (0, g, 0)),
            scratch_shapes=[pltpu.VMEM((128, 512), BF16)],
        ),
        compiler_params=pltpu.CompilerParams(vmem_limit_bytes=16 << 20),
        name="join_bins",
    )(meta, in_vmem(own), *[in_vmem(values) for values in pieces])


def per_device(
    first_homolog_embedding,
    second_homolog_embedding,
    token_chain_index,
    incoming_pair_state,
    tensor_mixing_matrix,
    outer_product_bias,
    transition_norm_gain,
    transition_gate_weight,
    transition_up_weight,
    transition_down_weight,
    distogram_weight,
    distogram_bias,
):
    row_at = lax.axis_index("row").astype(jnp.int32)
    col_at = lax.axis_index("col").astype(jnp.int32)
    meta = jnp.stack([row_at, col_at])

    left = jnp.transpose(first_homolog_embedding, (1, 2, 0)).reshape(1, 128, 128)
    right = jnp.transpose(second_homolog_embedding, (1, 2, 0)).reshape(1, 128, 128)

    centre = send(right, lambda a, b, c: (c, b, a))
    *weights, bin_col, chains = prep_call(
        tensor_mixing_matrix,
        transition_gate_weight,
        transition_up_weight,
        transition_down_weight,
        distogram_weight,
        outer_product_bias,
        transition_norm_gain,
        distogram_bias,
        token_chain_index,
    )
    left_two = jnp.concatenate([left, send(left, lambda a, b, c: (a, b, c ^ 1))], 0)
    before = send(centre, lambda a, b, c: ((a + 1) % 8, b, c))
    after = send(centre, lambda a, b, c: ((a - 1) % 8, b, c))
    left_near = jnp.concatenate([left_two, send(left_two, lambda a, b, c: (a, b, c ^ 4))], 0)
    opposite = send(centre, lambda a, b, c: ((a + 4) % 8, b, c))
    low = send(jnp.concatenate([before, centre], 0), lambda a, b, c: ((a + 2) % 8, b, c))
    high = send(jnp.concatenate([centre, after], 0), lambda a, b, c: ((a - 2) % 8, b, c))
    left_far = send(left_near, lambda a, b, c: (a, b, c ^ 2))
    own = jnp.concatenate([opposite, low, before, centre, after, high], 0)
    other = send(own, lambda a, b, c: (a, b ^ 1, c))
    own_far = send(own, lambda a, b, c: (a, b ^ 2, c))

    pieces = []
    pair_out = None
    for flip in (False, True):
        if flip:
            other = send(own_far, lambda a, b, c: (a, b ^ 1, c))
            own = own_far
        outer = outer_call(meta, flip, token_chain_index, chains, left_near, left_far, own, other)
        for part_at in range(2):
            pair_out, sent = rows_call(
                meta, flip, part_at, outer, incoming_pair_state, weights, pair_out
            )
            pieces.append(send(sent, lambda a, b, c, x=2 * flip: (c, b ^ x, a)))
    arrived = []
    for piece in pieces:
        arrived += [piece, send(piece, lambda a, b, c: (a, b ^ 1, c))]

    own_bins = own_call(pair_out, weights[3], bin_col)
    logits = join_call(meta, own_bins, arrived)
    return (pair_out, logits)


def solution(mesh):
    placed = (
        P(None, ("row", "col"), None),
        P(None, ("row", "col"), None),
        P(),
        P("row", "col", None),
        P(),
        P(),
        P(),
        P(),
        P(),
        P(),
        P(),
        P(),
    )
    return jax.shard_map(
        per_device,
        mesh=mesh,
        in_specs=placed,
        out_specs=(P("row", "col", None), P(None, "row", "col")),
        check_vma=False,
    )
```

```python
import functools

import jax
import jax.numpy as jnp
from jax import lax
from jax.experimental import pallas as pl
from jax.experimental.pallas import tpu as pltpu
from jax.sharding import PartitionSpec as P


AXES = ("row", "col")
F32 = jnp.float32
BF16 = jnp.bfloat16
DEVICES = [(a, b, c) for a in range(8) for b in range(4) for c in range(8)]
COL_MASKS = (0, 1, 4, 5, 2, 3, 6, 7)


def in_vmem(values):
    return pltpu.with_memory_space_constraint(values, pltpu.VMEM)


VMEM_SPEC = pl.BlockSpec(memory_space=pltpu.VMEM)


def flat(a, b, c):
    return (a * 4 + b) * 8 + c


def send(values, target):
    pairs = [(flat(*here), flat(*target(*here))) for here in DEVICES]
    return lax.ppermute(values, AXES, pairs)


def dot_nt(left, right):
    return lax.dot_general(left, right, (((1,), (1,)), ((), ())), preferred_element_type=F32)


def dot_nn(left, right):
    return lax.dot_general(left, right, (((1,), (0,)), ((), ())), preferred_element_type=F32)


def square_eye():
    down = lax.broadcasted_iota(jnp.int32, (128, 128), 0)
    along = lax.broadcasted_iota(jnp.int32, (128, 128), 1)
    return (down == along).astype(F32).astype(BF16)


def turn(values):
    return jnp.transpose(values.astype(F32), (1, 0))


def prep_kernel(
    mix, gate, up, down_w, bins_w, outer_bias, gain, bin_bias, chain_in,
    mixing, gate_up, down, bins, bias_col, gain_col, bin_col, chains, wide,
):
    chains[...] = chain_in[...]
    wide[...] = mix[...].astype(F32)
    for block in range(8):
        parts = [wide[pl.ds(block * 4 + d, 32, stride=32), :] for d in range(4)]
        mixing[:, block * 128 : (block + 1) * 128] = turn(jnp.concatenate(parts, 0)).astype(BF16)
    for block in range(4):
        lanes = slice(block * 128, (block + 1) * 128)
        gate_up[block * 128 : (block + 1) * 128, :] = turn(gate[:, lanes]).astype(BF16)
        gate_up[512 + block * 128 : 512 + (block + 1) * 128, :] = turn(up[:, lanes]).astype(BF16)
        down[:, lanes] = turn(down_w[lanes, :]).astype(BF16)
    spread = jnp.broadcast_to(bins_w[...].astype(F32)[:, None, :], (64, 8, 128)).reshape(512, 128)
    which = lax.rem(lax.broadcasted_iota(jnp.int32, (512, 128), 0), 8)
    for one in range(8):
        bins[:, one * 128 : (one + 1) * 128] = jnp.where(which == one, spread, 0.0).astype(BF16)
    bias_col[...] = turn(jnp.broadcast_to(outer_bias[...], (128, 128)))
    gain_col[...] = turn(jnp.broadcast_to(gain[...], (128, 128)))
    bin_col[...] = turn(jnp.broadcast_to(bin_bias[...], (128, 64)))


def prep_call(mix, gate, up, down, bins, outer_bias, gain, bin_bias, chain_at):
    operands = (mix, gate, up, down, bins.T, outer_bias[None], gain[None], bin_bias[None])
    operands += (chain_at.reshape(8, 128),)
    return pl.pallas_call(
        prep_kernel,
        out_shape=(
            pltpu.VMEM((128, 1024), BF16),
            pltpu.VMEM((1024, 128), BF16),
            pltpu.VMEM((128, 512), BF16),
            pltpu.VMEM((512, 1024), BF16),
            pltpu.VMEM((128, 128), F32),
            pltpu.VMEM((128, 128), F32),
            pltpu.VMEM((64, 128), F32),
            pltpu.VMEM((8, 128), jnp.int32),
        ),
        out_specs=[VMEM_SPEC] * 8,
        scratch_shapes=[pltpu.VMEM((1024, 128), F32)],
        compiler_params=pltpu.CompilerParams(vmem_limit_bytes=16 << 20),
        name="prep",
    )(*[pltpu.with_memory_space_constraint(v, pltpu.HBM) for v in operands])


def half_of(row_at, flip):
    x_lo = lax.rem(lax.div(row_at, 2), 2)
    return 1 - x_lo if flip else x_lo


def outer_kernel(
    meta,
    chain_at,
    left_near,
    left_far,
    right_own,
    right_other,
    chains,
    outer,
    right,
    left,
    packed,
    *,
    flip,
):
    row_at, col_at = meta[0], meta[1]
    half_at = half_of(row_at, flip)
    z_at = lax.div(row_at, 4)
    core = lax.rem(row_at, 2)
    first_chain = chain_at[row_at * 32]
    last_chain = chain_at[row_at * 32 + 31]

    for step in range(8):
        place = lax.rem(z_at + (step + 4), 8)
        own_row = pl.multiple_of((core * 8 + place) * 128, 128)
        other_row = pl.multiple_of(((1 - core) * 8 + place) * 128, 128)
        right[pl.ds(own_row, 128), :] = right_own[step].astype(F32)
        right[pl.ds(other_row, 128), :] = right_other[step].astype(F32)

    paired = lax.broadcasted_iota(jnp.int32, (64, 128), 1) < 64
    token = lax.broadcasted_iota(jnp.int32, (64, 128), 0) + (col_at * 128 + half_at * 64)
    zeros = jnp.zeros((64, 128), BF16)

    def one_chain(chain, window, unroll):
        for step, mask in enumerate(COL_MASKS):
            place = jnp.bitwise_xor(col_at, mask)
            chunk = left_near[step] if step < 4 else left_far[step - 4]
            for t in range(4):
                of_row = chain_at[row_at * 32 + place * 4 + t]
                values = chunk[t * 32 : (t + 1) * 32, :]
                values = jnp.where(of_row == chain, values, jnp.zeros_like(values))
                at = pl.multiple_of((place * 2 + t // 2) * 32, 32)
                left[pl.ds(at, 32), (t % 2) * 128 : (t % 2) * 128 + 128] = values
        start = jnp.sum((chains[...] < chain).astype(F32)).astype(jnp.int32)
        stop = jnp.sum((chains[...] <= chain).astype(F32)).astype(jnp.int32)
        same = jnp.logical_and(token >= start, token < stop)
        scale = jnp.where(
            same,
            F32(1.0 / 128.0),
            jnp.where(paired, F32(1.0 / 64.0), F32(0.0)),
        ).astype(BF16)

        def channels(step, inner):
            weights = []
            for pair in range(unroll):
                blocks = []
                for half in range(2):
                    d = step * (2 * unroll) + pair * 2 + half
                    at = pl.multiple_of(d * 64, 64)
                    if window is None:
                        values = right[pl.ds(d, 64, stride=32), :].astype(BF16)
                        packed[pl.ds(at, 64), :] = values
                    else:
                        values = packed[pl.ds(at, 64), :]
                    values = values * scale
                    blocks.append(jnp.concatenate([values, zeros], 1))
                    blocks.append(jnp.concatenate([zeros, values], 1))
                weights.append(jnp.concatenate(blocks, 0))
            for pair in range(unroll):
                if window is None:
                    rows_in = left[...]
                else:
                    rows_in = left[pl.ds(pl.multiple_of(window * 256, 256), 256), :]
                product = dot_nt(rows_in, weights[pair]).astype(BF16)
                for ip in range(16 if window is None else 8):
                    quad = ip // 2 if window is None else window * 4 + ip // 2
                    for half in range(2):
                        at = pl.multiple_of((step * (2 * unroll) + pair * 2 + half) * 32, 32)
                        lanes = (ip % 2) * 128
                        piece = product[ip * 32 : (ip + 1) * 32, half * 128 : (half + 1) * 128]
                        if window is not None:
                            piece = piece + outer[quad, pl.ds(at, 32), lanes : lanes + 128]
                        outer[quad, pl.ds(at, 32), lanes : lanes + 128] = piece
            return inner

        lax.fori_loop(0, 16 // unroll, channels, 0)

    main_chain = chain_at[row_at * 32 + 16]
    one_chain(main_chain, None, 4)

    def more_chains(step, carry):
        chain = step + (step >= main_chain).astype(jnp.int32)
        one_chain(chain, (chain > main_chain).astype(jnp.int32), 4)
        return carry

    lax.fori_loop(first_chain, last_chain, more_chains, 0)


def outer_call(meta, flip, chain_at, chains, left_near, left_far, own, other):
    operands = [left_near, left_far, own, other, chains]
    return pl.pallas_call(
        functools.partial(outer_kernel, flip=flip),
        out_shape=pltpu.VMEM((8, 1024, 256), BF16),
        grid_spec=pltpu.PrefetchScalarGridSpec(
            num_scalar_prefetch=2,
            grid=(1,),
            in_specs=[VMEM_SPEC] * len(operands),
            out_specs=VMEM_SPEC,
            scratch_shapes=[
                pltpu.VMEM((2048, 128), F32),
                pltpu.VMEM((512, 256), BF16),
                pltpu.VMEM((2048, 128), BF16),
            ],
        ),
        compiler_params=pltpu.CompilerParams(vmem_limit_bytes=12 << 20),
        name="outer_half",
    )(
        meta,
        pltpu.with_memory_space_constraint(chain_at, pltpu.HBM),
        *[in_vmem(values) for values in operands],
    )


def rows_kernel(
    meta, outer, incoming, mixing, gate_up, down, bins, bias_col, gain_col, *rest, flip, part_at
):
    out, sent, tile, rows = rest[-4:]
    row_at = meta[0]
    core = lax.rem(row_at, 2)
    half_at = half_of(row_at, flip)
    eye = square_eye()
    bias = jnp.concatenate([bias_col[...], bias_col[...]], 1)
    scale_by = jnp.concatenate([gain_col[...], gain_col[...]], 1)

    def mixed(quad):
        arriving = incoming[
            pl.ds(pl.multiple_of(part_at * 16 + quad * 4, 4), 4),
            pl.ds(pl.multiple_of(half_at * 64, 64), 64),
            :,
        ].reshape(256, 128)
        mid = dot_nn(mixing[...], outer[part_at * 4 + quad]) + dot_nt(eye, arriving) + bias
        return mid.astype(BF16).astype(F32)

    def normalised(mid):
        center = jnp.sum(mid, axis=0, keepdims=True) * F32(1.0 / 128.0)
        shifted = mid - center
        spread = jnp.sum(shifted * shifted, axis=0, keepdims=True) * F32(1.0 / 128.0)
        return (shifted * lax.rsqrt(spread + F32(1e-05)) * scale_by).astype(BF16)

    def widened(normed, part):
        gate = dot_nn(gate_up[part * 256 : (part + 1) * 256, :], normed)
        up = dot_nn(gate_up[512 + part * 256 : 512 + (part + 1) * 256, :], normed)
        half_gate = gate * F32(0.5)
        return ((half_gate + half_gate * jnp.tanh(half_gate)) * up).astype(BF16)

    def narrowed(hidden, part):
        return dot_nn(down[:, part * 256 : (part + 1) * 256], hidden)

    def finish(quad, result):
        turned = turn(result.astype(BF16))
        out[quad * 4 : quad * 4 + 4] = turned.astype(BF16).reshape(4, 64, 128)
        tile[quad * 256 : (quad + 1) * 256, :] = turned

    mid = mixed(0)
    normed = normalised(mid)
    for quad in range(4):
        following = mixed(quad + 1) if quad + 1 < 4 else None
        result = mid
        hidden = widened(normed, 0)
        for part in range(1, 2):
            ahead = widened(normed, part)
            result = result + narrowed(hidden, part - 1)
            hidden = ahead
        if following is not None:
            normed = normalised(following)
        result = result + narrowed(hidden, 1)
        finish(quad, result)
        mid = following

    for group in range(8):
        for one in range(8):
            values = tile[pl.ds(group * 8 + one, 16, stride=64), :].astype(BF16)
            rows[group * 16 : (group + 1) * 16, one * 128 : (one + 1) * 128] = values
    product = dot_nt(rows[...], bins[...]).astype(BF16).reshape(2, 4, 16, 512)
    sent[core] = product[0]
    sent[1 - core] = product[1]


def rows_call(meta, flip, part_at, outer, incoming, weights, so_far):
    block = pl.BlockSpec((16, 64, 128), lambda g, m: (part_at, half_of(m[0], flip), 0))
    operands = [in_vmem(values) for values in (outer, incoming, *weights)]
    specs = [VMEM_SPEC] * len(operands)
    aliases = {}
    if so_far is not None:
        operands.append(so_far)
        specs.append(pl.BlockSpec(memory_space=pl.ANY))
        aliases = {len(operands): 0}
    return pl.pallas_call(
        functools.partial(rows_kernel, flip=flip, part_at=part_at),
        out_shape=(
            jax.ShapeDtypeStruct((32, 128, 128), BF16),
            pltpu.VMEM((2, 4, 16, 512), BF16),
        ),
        grid_spec=pltpu.PrefetchScalarGridSpec(
            num_scalar_prefetch=1,
            grid=(1,),
            in_specs=specs,
            out_specs=(block, VMEM_SPEC),
            scratch_shapes=[pltpu.VMEM((1024, 128), F32), pltpu.VMEM((128, 1024), BF16)],
        ),
        input_output_aliases=aliases,
        compiler_params=pltpu.CompilerParams(vmem_limit_bytes=12 << 20),
        name="rows_part",
    )(meta, *operands)


def own_kernel(tile, bins, bias, out):
    rows = pl.ds(pl.multiple_of(pl.program_id(0) * 8, 8), 8)
    flat_rows = jnp.concatenate([tile[i] for i in range(8)], axis=1)
    product = dot_nt(bins[...], flat_rows).astype(BF16).astype(F32)
    out[:, rows, :] = product.reshape(64, 8, 128) + bias[...][:, None, :]


def own_call(pair_out, bins, bias):
    return pl.pallas_call(
        own_kernel,
        out_shape=pltpu.VMEM((64, 32, 128), F32),
        grid=(4,),
        in_specs=[pl.BlockSpec((8, 128, 128), lambda g: (g, 0, 0)), VMEM_SPEC, VMEM_SPEC],
        out_specs=VMEM_SPEC,
        compiler_params=pltpu.CompilerParams(vmem_limit_bytes=16 << 20),
        name="own_bins",
    )(pair_out, in_vmem(bins), in_vmem(bias))


def join_kernel(meta, own, *rest):
    out, block = rest[-2:]
    b_at = lax.rem(meta[0], 4)
    step = pl.program_id(0)
    eye = square_eye()
    for group in range(2):
        rows = pl.ds(pl.multiple_of(step * 16 + group * 8, 8), 8)
        for piece in range(4):
            for side in range(2):
                values = rest[piece * 2 + side]
                from_b = jnp.bitwise_xor(b_at, (piece // 2) * 2 + side)
                at = pl.multiple_of(from_b * 32 + (piece % 2) * 16, 16)
                block[group, pl.ds(at, 16), :] = values[side, step * 2 + group]
        for part in range(4):
            turned = dot_nt(eye, block[group, :, part * 128 : (part + 1) * 128])
            out[part * 16 : (part + 1) * 16, group * 8 : (group + 1) * 8, :] = own[
                part * 16 : (part + 1) * 16, rows, :
            ] + turned.reshape(16, 8, 128)


def join_call(meta, own, pieces):
    return pl.pallas_call(
        join_kernel,
        out_shape=jax.ShapeDtypeStruct((64, 32, 128), F32),
        grid_spec=pltpu.PrefetchScalarGridSpec(
            num_scalar_prefetch=1,
            grid=(2,),
            in_specs=[VMEM_SPEC] * 9,
            out_specs=pl.BlockSpec((64, 16, 128), lambda g, m: (0, g, 0)),
            scratch_shapes=[pltpu.VMEM((2, 128, 512), BF16)],
        ),
        compiler_params=pltpu.CompilerParams(vmem_limit_bytes=16 << 20),
        name="join_bins",
    )(meta, in_vmem(own), *[in_vmem(values) for values in pieces])


def per_device(
    first_homolog_embedding,
    second_homolog_embedding,
    token_chain_index,
    incoming_pair_state,
    tensor_mixing_matrix,
    outer_product_bias,
    transition_norm_gain,
    transition_gate_weight,
    transition_up_weight,
    transition_down_weight,
    distogram_weight,
    distogram_bias,
):
    row_at = lax.axis_index("row").astype(jnp.int32)
    col_at = lax.axis_index("col").astype(jnp.int32)
    meta = jnp.stack([row_at, col_at])

    left = jnp.transpose(first_homolog_embedding, (1, 2, 0)).reshape(1, 128, 128)
    right = jnp.transpose(second_homolog_embedding, (1, 2, 0)).reshape(1, 128, 128)

    centre = send(right, lambda a, b, c: (c, b, a))
    *weights, bin_col, chains = prep_call(
        tensor_mixing_matrix,
        transition_gate_weight,
        transition_up_weight,
        transition_down_weight,
        distogram_weight,
        outer_product_bias,
        transition_norm_gain,
        distogram_bias,
        token_chain_index,
    )
    left_two = jnp.concatenate([left, send(left, lambda a, b, c: (a, b, c ^ 1))], 0)
    before = send(centre, lambda a, b, c: ((a + 1) % 8, b, c))
    after = send(centre, lambda a, b, c: ((a - 1) % 8, b, c))
    left_near = jnp.concatenate([left_two, send(left_two, lambda a, b, c: (a, b, c ^ 4))], 0)
    opposite = send(centre, lambda a, b, c: ((a + 4) % 8, b, c))
    low = send(jnp.concatenate([before, centre], 0), lambda a, b, c: ((a + 2) % 8, b, c))
    high = send(jnp.concatenate([centre, after], 0), lambda a, b, c: ((a - 2) % 8, b, c))
    left_far = send(left_near, lambda a, b, c: (a, b, c ^ 2))
    own = jnp.concatenate([opposite, low, before, centre, after, high], 0)
    other = send(own, lambda a, b, c: (a, b ^ 1, c))
    own_far = send(own, lambda a, b, c: (a, b ^ 2, c))

    pieces = []
    pair_out = None
    for flip in (False, True):
        if flip:
            other = send(own_far, lambda a, b, c: (a, b ^ 1, c))
            own = own_far
        outer = outer_call(meta, flip, token_chain_index, chains, left_near, left_far, own, other)
        for part_at in range(2):
            pair_out, sent = rows_call(
                meta, flip, part_at, outer, incoming_pair_state, weights, pair_out
            )
            pieces.append(send(sent, lambda a, b, c, x=2 * flip: (c, b ^ x, a)))
    arrived = []
    for piece in pieces:
        arrived += [piece, send(piece, lambda a, b, c: (a, b ^ 1, c))]

    own_bins = own_call(pair_out, weights[3], bin_col)
    logits = join_call(meta, own_bins, arrived)
    return (pair_out, logits)


def solution(mesh):
    placed = (
        P(None, ("row", "col"), None),
        P(None, ("row", "col"), None),
        P(),
        P("row", "col", None),
        P(),
        P(),
        P(),
        P(),
        P(),
        P(),
        P(),
        P(),
    )
    return jax.shard_map(
        per_device,
        mesh=mesh,
        in_specs=placed,
        out_specs=(P("row", "col", None), P(None, "row", "col")),
        check_vma=False,
    )
```
